32 devices in a mesh: groups: 2 (over y), visit: 4 (over z), strip: 2 (over x), band: 2 (over core).
Axes of the slice: x: 2, y: 2, z: 4, core: 2. Of those that a mesh axis runs over, the one named last changes fastest.
Arguments:
- images: bfloat16 [2, 128, 128, 256], P('band', ('groups', 'visit'), 'strip'), parts along dimension 1, may hold values from -8 to 8
- mask_bits: int32 [2, 128, 128, 256], P('band', ('groups', 'visit'), 'strip'), parts along dimension 1, may hold values from 0 to 15
- visit_weight: bfloat16 [2, 128], P('band', ('groups', 'visit')), parts along dimension 1, may hold values from 1 to 4
- intersection: int32 [128, 1], P(('groups', 'visit')), parts along dimension 0, may hold values from 0 to 3, as said below
- patch_owner: int32 [8], P('groups'), parts along dimension 0, may hold values from 0 to 3, each once
Outputs:
- coadd_image: bfloat16 [2, 8, 128, 256], P('band', ('groups', 'visit'), 'strip'), parts along dimension 1
- difference: bfloat16 [2, 128, 128, 256], P('band', ('groups', 'visit'), 'strip'), parts along dimension 1
The draws below stay inside these ranges and needn't reach their ends.
There are 2 independent parts, one for each index of `groups`. The reference program is written for one: setup_inputs(seed, part) draws one part's arguments, and reference() takes and returns one part's arrays. A program takes and returns all parts, laid end to end along the dimension named above; each array names one. Nothing has to cross between parts.
Inputs may be any that keep to these rules, and one draw needn't show every extreme that they name: `intersection`: row j names the patch that piece j intersections. The 16 pieces of one visit index intersect 16 // 8 distinct patches, exactly 8 pieces each; one patch is intersected by 8 pieces of every visit index, and every patch is intersected by some piece. `patch_owner`: A permutation of the patches.
All inputs are finite; a program needn't handle non-finite values.
Results may differ from the reference program's by a relative error of at most 0.0071.
Values may be sent and summed in bfloat16 or wider, within the bound.
A program may use at most 64 MiB of HBM per device.

```python
import math
import jax
import jax.numpy as jnp
from jax import lax

COLS = 256
PIECES_DEV = 16
CAP = 8
BASES = 6
HALF = 9
PATCHES = 4
PIECES = 64
ROWS = 128
BANDS = 2


basis_rows = (0, 0, 1, 0, 2, 1)


basis_cols = (0, 1, 0, 2, 0, 1)


def tap_rows():
    offsets = jnp.arange(2 * HALF + 1).astype(jnp.float32) - HALF
    gaussian = jnp.exp(-offsets * offsets / 18.0)
    centre = jnp.sum(offsets * offsets * gaussian * gaussian) / jnp.sum(gaussian * gaussian)
    tap_table = jnp.stack([gaussian, offsets * gaussian, (offsets * offsets - centre) * gaussian])
    return tap_table / jnp.sqrt(jnp.sum(tap_table * tap_table, axis=1, keepdims=True))


def intersection_table(key):
    base_key = jax.random.fold_in(key, 7001)
    ranking_key, turn_key, order_key = jax.random.split(base_key, 3)
    ranking = jax.random.permutation(ranking_key, PATCHES).astype(jnp.int32)
    rotate = jax.random.randint(turn_key, (), 0, PATCHES - 1).astype(jnp.int32)
    position = jnp.arange(PIECES).astype(jnp.int32)
    visit_index = position // PIECES_DEV
    local_index = position % PIECES_DEV
    group = local_index // CAP
    rank_index = jnp.where(group == 0, 0, 1 + (rotate + visit_index + group - 1) % (PATCHES - 1))
    ordered = ranking[rank_index]

    def shuffle_block(block_key):
        return jax.random.permutation(block_key, PIECES_DEV).astype(jnp.int32)
    shuffles = jax.vmap(shuffle_block)(jax.random.split(order_key, PATCHES))
    chosen = (jnp.arange(PATCHES).astype(jnp.int32)[:, None] * PIECES_DEV + shuffles).reshape(PIECES)
    return ordered[chosen].astype(jnp.int32)


def draw_intersection(key, part):
    return intersection_table(key)[:, None]


def draw_images(key, part):
    patch_ids = intersection_table(key)
    base_key = jax.random.fold_in(key, 7103)
    sky_key, mixing_key, noise_key, scale_key = jax.random.split(base_key, 4)
    sky_field = jax.random.normal(sky_key, (BANDS, PATCHES, ROWS, COLS), jnp.float32)
    taps = tap_rows()
    padded = jnp.pad(sky_field, ((0, 0), (0, 0), (HALF, HALF), (0, 0)))
    vertical = jnp.zeros((3, BANDS, PATCHES, ROWS, COLS), jnp.float32)
    for offset_index in range(2 * HALF + 1):
        vertical = vertical + taps[:, offset_index, None, None, None, None] * padded[None, :, :, offset_index:offset_index + ROWS]
    widened = jnp.pad(vertical, ((0, 0), (0, 0), (0, 0), (0, 0), (HALF, HALF)))
    plane_list = []
    for basis_index in range(BASES):
        total = jnp.zeros((BANDS, PATCHES, ROWS, COLS), jnp.float32)
        for offset_index in range(2 * HALF + 1):
            total = total + taps[basis_cols[basis_index], offset_index] * widened[basis_rows[basis_index], :, :, :, offset_index:offset_index + COLS]
        plane_list.append(total)
    planes = jnp.stack(plane_list)
    mixing = 0.5 * jax.random.normal(mixing_key, (PIECES, BASES), jnp.float32)

    def one_piece(piece_index):
        patch = patch_ids[piece_index]
        sky_plane = lax.dynamic_index_in_dim(sky_field, patch, 1, keepdims=False)
        convolved = lax.dynamic_index_in_dim(planes, patch, 2, keepdims=False)
        piece_key = jax.random.fold_in(noise_key, piece_index)
        noise = 0.3 * jax.random.normal(piece_key, (BANDS, ROWS, COLS), jnp.float32)
        mixed = jnp.sum(mixing[piece_index][:, None, None, None] * convolved, axis=0)
        return sky_plane + mixed + noise
    pieces_all = lax.map(one_piece, jnp.arange(PIECES).astype(jnp.int32))
    result = jnp.clip(jnp.transpose(pieces_all, (1, 0, 2, 3)), -8.0, 8.0)
    return result.astype(jnp.bfloat16)


def set_ends(entries, key, smallest, high):
    extent = entries.shape
    spot = [jax.random.randint(jax.random.fold_in(key, axis), (), 0, extent[axis]) for axis in range(len(extent))]
    entries = entries.at[tuple(spot)].set(smallest)
    longest = extent.index(max(extent))
    spot[longest] = (spot[longest] + 1) % extent[longest]
    return entries.at[tuple(spot)].set(high)


def block_scale(key, dims, shards, smallest, top_value):
    def one(dim, blocks):
        draws = jax.random.uniform(jax.random.fold_in(jax.random.fold_in(key, 6), dim), (blocks,), jnp.float32, smallest / len(shards), top_value / len(shards))
        return jnp.repeat(jnp.exp(draws), dims[dim] // blocks).reshape((-1,) + (1,) * (len(dims) - dim - 1))

    loudness = one(*shards[0])
    for cut in shards[1:]:
        loudness = loudness * one(*cut)
    return loudness


def setup_inputs(seed: int = 0, part: int = 0) -> dict:
    arg_keys = jax.random.split(jax.random.key(seed), 6)
    part_splits = jax.random.split(jax.random.fold_in(arg_keys[5], part), 6)
    return {
        "images": draw_images(jax.random.fold_in(jax.random.fold_in(arg_keys[5], part), 71), part),
        "mask_bits": set_ends(jax.random.randint(part_splits[1], (BANDS, PIECES, ROWS, COLS), 0, 16), jax.random.fold_in(part_splits[1], 1), 0, 15).astype(jnp.int32),
        "visit_weight": jnp.clip(jnp.exp(math.log(4.0) - 1.3862944 * jax.random.uniform(part_splits[2], (BANDS, PIECES), jnp.float32) ** block_scale(part_splits[2], (BANDS, PIECES), ((0, 2), (1, 4)), -0.2, 0.2)), 1.0, 4.0).astype(jnp.bfloat16),
        "intersection": draw_intersection(jax.random.fold_in(jax.random.fold_in(arg_keys[5], part), 71), part),
        "patch_owner": jax.random.permutation(part_splits[4], PATCHES).astype(jnp.int32),
    }


basis_rows = (0, 0, 1, 0, 2, 1)
basis_cols = (0, 1, 0, 2, 0, 1)

def kernel_taps():
    offsets = jnp.arange(2 * HALF + 1).astype(jnp.float32) - HALF
    gaussian = jnp.exp(-offsets * offsets / 18.0)
    centre = jnp.sum(offsets * offsets * gaussian * gaussian) / jnp.sum(gaussian * gaussian)
    tap_table = jnp.stack([gaussian, offsets * gaussian, (offsets * offsets - centre) * gaussian])
    tap_table = tap_table / jnp.sqrt(lax.optimization_barrier(jnp.sum(tap_table * tap_table, axis=1, keepdims=True)))
    return tap_table.astype(jnp.bfloat16)

def solve_small(matrix, right_side):
    dimension = matrix.shape[-1]
    augmented = jnp.concatenate([matrix, right_side[..., None]], axis=-1)
    for column in range(dimension):
        pivot_row = augmented[..., column, :] / augmented[..., column, column:column + 1]
        augmented = augmented - augmented[..., :, column:column + 1] * pivot_row[..., None, :]
        augmented = augmented.at[..., column, :].set(pivot_row)
    return augmented[..., :, dimension]

def reference(images, mask_bits, visit_weight, intersection, patch_owner):
    usable = (jnp.bitwise_and(mask_bits, 3) != 3).astype(jnp.bfloat16)
    weighted = visit_weight[:, :, None, None] * usable
    patch_ids = intersection[:, 0]
    band_count = images.shape[0]
    zero_planes = jnp.zeros((band_count, PATCHES, ROWS, COLS), jnp.float32)

    def accumulate(carry, piece_index):
        numerator, denominator = carry
        weight_plane = lax.dynamic_index_in_dim(weighted, piece_index, 1, keepdims=False).astype(jnp.float32)
        image_plane = lax.dynamic_index_in_dim(images, piece_index, 1, keepdims=False).astype(jnp.float32)
        target = patch_ids[piece_index]
        numerator = numerator.at[:, target].add(weight_plane * image_plane)
        denominator = denominator.at[:, target].add(weight_plane)
        return ((numerator, denominator), None)
    (numerator, denominator), _ = lax.scan(accumulate, (zero_planes, zero_planes), jnp.arange(PIECES))
    coadd_patch = (numerator / jnp.maximum(denominator, 1.0)).astype(jnp.bfloat16)
    coadd_image = jnp.zeros_like(coadd_patch).at[:, patch_owner].set(coadd_patch)
    taps_float = kernel_taps().astype(jnp.float32)

    def per_piece(piece_index):
        template = jnp.take(coadd_patch, patch_ids[piece_index], axis=1).astype(jnp.float32)
        padded = jnp.pad(template, ((0, 0), (HALF, HALF), (0, 0)))
        smooth = jnp.zeros((3, band_count, ROWS, COLS), jnp.float32)
        for offset_index in range(2 * HALF + 1):
            smooth = smooth + taps_float[:, offset_index, None, None, None] * padded[None, :, offset_index:offset_index + ROWS]
        smooth = smooth.astype(jnp.bfloat16)
        widened = jnp.pad(smooth.astype(jnp.float32), ((0, 0), (0, 0), (0, 0), (HALF, HALF)))
        planes = []
        for basis_index in range(BASES):
            total = jnp.zeros((band_count, ROWS, COLS), jnp.float32)
            for offset_index in range(2 * HALF + 1):
                total = total + taps_float[basis_cols[basis_index], offset_index] * widened[basis_rows[basis_index], :, :, offset_index:offset_index + COLS]
            planes.append(total.astype(jnp.bfloat16))
        basis = jnp.stack(planes).astype(jnp.float32)
        usable_plane = lax.dynamic_index_in_dim(usable, piece_index, 1, keepdims=False).astype(jnp.float32)
        science = lax.dynamic_index_in_dim(images, piece_index, 1, keepdims=False).astype(jnp.float32)
        masked = basis * usable_plane[None]
        normal = jnp.einsum('abyx,cbyx->bac', masked, basis, precision=lax.Precision.HIGHEST)
        right_side = jnp.einsum('abyx,byx->ba', masked, science, precision=lax.Precision.HIGHEST)
        coefficients = solve_small(normal + jnp.eye(BASES, dtype=jnp.float32), right_side)
        fitted = jnp.einsum('ba,abyx->byx', coefficients, basis, precision=lax.Precision.HIGHEST)
        return (science - fitted).astype(jnp.bfloat16)
    difference = jnp.transpose(lax.map(per_piece, jnp.arange(PIECES)), (1, 0, 2, 3))
    return (coadd_image, difference)
```

```python
import functools

import jax
import jax.numpy as jnp
import numpy as np
from jax import lax
from jax.experimental import pallas as pl
from jax.experimental.pallas import tpu as pltpu
from jax.sharding import PartitionSpec as P

BASES = 6
HALF = 9
TILE = 16
LANES = 128

basis_rows = (0, 0, 1, 0, 2, 1)
basis_cols = (0, 1, 0, 2, 0, 1)
pairs = tuple((a, c) for a in range(BASES) for c in range(a, BASES))
MESH = pl.DeviceIdType.MESH
F32 = jnp.float32
BF16 = jnp.bfloat16


def kernel_taps():
    offsets = np.arange(2 * HALF + 1).astype(np.float32) - HALF
    gaussian = np.exp(-offsets * offsets / np.float32(18.0))
    centre = np.sum(offsets * offsets * gaussian * gaussian) / np.sum(gaussian * gaussian)
    table = np.stack([gaussian, offsets * gaussian, (offsets * offsets - centre) * gaussian])
    table = table / np.sqrt(np.sum(table * table, axis=1, keepdims=True))
    return table.astype(BF16).astype(np.float32)


def band_matrix(table, lead, trail, displace):
    index = np.arange(trail)[None, :] - np.arange(lead)[:, None] + displace
    inside = (index >= 0) & (index <= 2 * HALF)
    return np.where(inside[None], table[:, np.clip(index, 0, 2 * HALF)], 0.0)


def gather_matrix():
    result = np.zeros(((len(pairs) + BASES) * TILE, LANES), np.float32)
    for n, (a, c) in enumerate(pairs):
        result[n * TILE : (n + 1) * TILE, a * 8 + c] = 1.0
        result[n * TILE : (n + 1) * TILE, c * 8 + a] = 1.0
    for a in range(BASES):
        n = len(pairs) + a
        result[n * TILE : (n + 1) * TILE, a * 8 + 6] = 1.0
    return result


def iota(shape, dim):
    return lax.broadcasted_iota(jnp.int32, shape, dim)


def nn(a, b):
    return jnp.dot(a, b, preferred_element_type=F32)


def nt(a, b):
    return lax.dot_general(a, b, (((1,), (1,)), ((), ())), preferred_element_type=F32)


def tn(a, b):
    return lax.dot_general(a, b, (((0,), (0,)), ((), ())), preferred_element_type=F32)


def each(count, step):
    if count <= 4:
        for k in range(count):
            step(k)
    else:
        def body(k, carry):
            step(k)
            return carry

        lax.fori_loop(0, count, body, 0)


def thirds(value):
    high = value.astype(BF16)
    rest = value - high.astype(F32)
    middle = rest.astype(BF16)
    low = (rest - middle.astype(F32)).astype(BF16)
    return jnp.concatenate([high, middle, low], axis=0)


def kernel(
    visits, strips, distinct,
    images, masks, weight_in, cross_in, owner_in, table_in,
    coadd_out, image_v, basis, mixers,
    mask_v, tables, weight, cross, cross_scalar, owner, use, use_image, send, recv, ids_own, ids,
    patches, chosen, template_v, owned, prods, small, small_in,
    in_sem, const_sem, first_sem, rs_send, rs_recv, id_send, id_recv, ag_send, ag_recv,
    halo_send, halo_recv, own_send, own_recv, st_send, st_recv,
):
    pieces, rows, cols = images.shape[1:]
    blocks = rows // TILE
    span = pieces * TILE
    halves = cols // LANES
    lead = (visits - halves) // 2
    me = lax.axis_index("visit")
    strip = lax.axis_index("strip")
    above = strip > 0
    below = strip < strips - 1

    firsts = [
        pltpu.make_async_copy(cross_in, cross_scalar, first_sem.at[0]),
        pltpu.make_async_copy(owner_in, owner, first_sem.at[1]),
        pltpu.make_async_copy(cross_in, cross, first_sem.at[2]),
        pltpu.make_async_copy(weight_in, weight, first_sem.at[3]),
    ]
    for copy in firsts:
        copy.start()

    barrier = pltpu.get_barrier_semaphore()
    for k in range(visits):
        for hop in range(strips):
            if k == 0 and hop == 0:
                continue
            target = {"visit": lax.rem(me + k, visits), "strip": lax.rem(strip + hop, strips)}
            pl.semaphore_signal(barrier, inc=1, device_id=target, device_id_type=MESH)

    loads = []
    for t in range(blocks):
        piece_rows = pl.ds(t * TILE, TILE)
        loads.append((
            pltpu.make_async_copy(masks.at[0, :, piece_rows, :], mask_v.at[t], in_sem.at[0, t]),
            pltpu.make_async_copy(images.at[0, :, piece_rows, :], image_v.at[t], in_sem.at[1, t]),
        ))
        for copy in loads[t]:
            copy.start()
    constants = pltpu.make_async_copy(table_in, tables, const_sem)
    constants.start()

    for copy in firsts:
        copy.wait()
    seats = [owner[cross_scalar[0, j]] for j in range(pieces)]
    slots = [jnp.int32(0)] * distinct
    rank = jnp.int32(0)
    for q in range(visits):
        present = jnp.int32(0)
        for j in range(pieces):
            present = present | jnp.where(seats[j] == q, 1, 0)
        for d in range(distinct):
            slots[d] = slots[d] + jnp.where((present == 1) & (rank == d), q, 0)
        rank = rank + present

    position = jnp.zeros((1, pieces), jnp.int32)
    for p in range(visits):
        position = position + jnp.where(cross[...] == p, owner[p], 0)
    e2 = iota((pieces, span), 0) == jnp.right_shift(iota((pieces, span), 1), 4)
    e2 = e2.astype(F32).astype(BF16)
    pair = jnp.where(
        iota((8, pieces), 0) == 0, weight[...].astype(F32), position.astype(F32)
    ).astype(BF16)
    wide = nn(pair, e2)
    same = (iota((TILE, span), 0) & (TILE - 1)) == (iota((TILE, span), 1) & (TILE - 1))
    adder = jnp.concatenate([
        jnp.where(same & (wide[1:2] == lax.convert_element_type(slots[d], F32)), wide[0:1], 0.0)
        for d in range(distinct)
    ], axis=0).astype(BF16)

    for t in range(blocks):
        for copy in loads[t]:
            copy.wait()
        usable = ((mask_v[t].reshape(span, cols) & 3) != 3).astype(F32).astype(BF16)
        masked = usable * image_v[t].reshape(span, cols)
        lanes = pl.ds(t * cols, cols)
        use[:, lanes] = usable
        use_image[:, lanes] = masked
        for part, value in enumerate((masked, usable)):
            total = nn(adder, value).astype(BF16)
            for d in range(distinct):
                for h in range(halves):
                    send[h, d, part, pl.ds(t * TILE, TILE), :] = total[
                        d * TILE : (d + 1) * TILE, h * LANES : (h + 1) * LANES
                    ]
    names = jnp.zeros((1, LANES), jnp.int32)
    for d in range(distinct):
        names = names + jnp.where(iota((1, LANES), 1) == d, slots[d], 0)
    ids_own[...] = names.astype(F32)

    def sum_copies(h, source):
        return (
            pltpu.make_async_remote_copy(
                src_ref=ids_own, dst_ref=ids.at[source],
                send_sem=id_send.at[h], recv_sem=id_recv.at[source],
                device_id={"visit": lead + h}, device_id_type=MESH,
            ),
            pltpu.make_async_remote_copy(
                src_ref=send.at[h], dst_ref=recv.at[source],
                send_sem=rs_send.at[h], recv_sem=rs_recv.at[source],
                device_id={"visit": lead + h}, device_id_type=MESH,
            ),
        )

    def template_copy(h, v, d):
        return pltpu.make_async_remote_copy(
            src_ref=chosen.at[v, d], dst_ref=template_v.at[d, h, pl.ds(TILE, rows), :],
            send_sem=ag_send.at[v, d], recv_sem=ag_recv.at[h, d],
            device_id={"visit": v}, device_id_type=MESH,
        )

    def edge_copy(way, h, v, d):
        step, source, target = ((1, rows - TILE, 0), (strips - 1, 0, rows + TILE))[way]
        return pltpu.make_async_remote_copy(
            src_ref=chosen.at[v, d, pl.ds(source, TILE), :],
            dst_ref=template_v.at[d, h, pl.ds(target, TILE), :],
            send_sem=halo_send.at[way, v, d], recv_sem=halo_recv.at[way, h, d],
            device_id={"visit": v, "strip": lax.rem(strip + step, strips)}, device_id_type=MESH,
        )

    def owned_copy(h, v):
        return pltpu.make_async_remote_copy(
            src_ref=patches.at[v], dst_ref=owned.at[h],
            send_sem=own_send.at[v], recv_sem=own_recv.at[h],
            device_id={"visit": v}, device_id_type=MESH,
        )

    pl.semaphore_wait(barrier, visits * strips - 1)
    for h in range(halves):
        @pl.when(me != lead + h)
        def _():
            for copy in sum_copies(h, me):
                copy.start()

    @pl.when(jnp.logical_not(above))
    def _():
        template_v[:, :, pl.ds(0, TILE), :] = jnp.zeros((distinct, halves, TILE, LANES), BF16)

    @pl.when(jnp.logical_not(below))
    def _():
        template_v[:, :, pl.ds(rows + TILE, TILE), :] = jnp.zeros(
            (distinct, halves, TILE, LANES), BF16
        )

    mine = me - lead
    owning = (me >= lead) & (me < lead + halves)

    def id_tile(v, d):
        return jnp.broadcast_to(ids[v][:, d : d + 1], (TILE, LANES))

    def reduce():
        recv[me] = send[mine]
        ids[me] = ids_own[...]
        for v in range(visits):
            @pl.when(me != v)
            def _():
                for copy in sum_copies(0, v):
                    copy.wait_recv()

        def one_tile(t):
            piece_rows = pl.ds(t * TILE, TILE)
            if visits <= 4:
                tiles = [[id_tile(v, d) for d in range(distinct)] for v in range(visits)]
                finals = []
                for q in range(visits):
                    numerator = jnp.zeros((TILE, LANES), F32)
                    denominator = jnp.zeros((TILE, LANES), F32)
                    for v in range(visits):
                        for d in range(distinct):
                            here = tiles[v][d] == float(q)
                            numerator += jnp.where(
                                here, recv[v, d, 0, piece_rows, :].astype(F32), 0.0
                            )
                            denominator += jnp.where(
                                here, recv[v, d, 1, piece_rows, :].astype(F32), 0.0
                            )
                    final = numerator / jnp.maximum(denominator, 1.0)
                    patches[q, piece_rows, :] = final.astype(BF16)
                    finals.append(final)
                for v in range(visits):
                    for d in range(distinct):
                        picked = finals[0]
                        for q in range(1, visits):
                            picked = jnp.where(tiles[v][d] == float(q), finals[q], picked)
                        chosen[v, d, piece_rows, :] = picked.astype(BF16)
                return

            def one_patch(q):
                number = lax.convert_element_type(q, F32)

                def add(v, carry):
                    numerator, denominator = carry
                    for d in range(distinct):
                        here = id_tile(v, d) == number
                        numerator += jnp.where(here, recv[v, d, 0, piece_rows, :].astype(F32), 0.0)
                        denominator += jnp.where(here, recv[v, d, 1, piece_rows, :].astype(F32), 0.0)
                    return numerator, denominator

                zero = jnp.zeros((TILE, LANES), F32)
                numerator, denominator = lax.fori_loop(0, visits, add, (zero, zero))
                final = numerator / jnp.maximum(denominator, 1.0)
                patches[q, piece_rows, :] = final.astype(BF16)

            def pick(v):
                for d in range(distinct):
                    tile = id_tile(v, d)

                    def better(q, picked):
                        final = patches[q, piece_rows, :].astype(F32)
                        return jnp.where(tile == lax.convert_element_type(q, F32), final, picked)

                    picked = lax.fori_loop(0, visits, better, jnp.zeros((TILE, LANES), F32))
                    chosen[v, d, piece_rows, :] = picked.astype(BF16)

            each(visits, one_patch)
            each(visits, pick)

        for t in range(blocks):
            one_tile(t)

        for d in range(distinct):
            def templates(v):
                pl.when(below)(edge_copy(0, mine, v, d).start)
                pl.when(above)(edge_copy(1, mine, v, d).start)

                @pl.when(me != v)
                def _():
                    template_copy(mine, v, d).start()

            each(visits, templates)

        def owners(v):
            @pl.when(me != v)
            def _():
                owned_copy(mine, v).start()

        each(visits, owners)
        template_v[:, mine, pl.ds(TILE, rows), :] = chosen[me]
        owned[mine] = patches[me]

    pl.when(owning)(reduce)
    constants.wait()

    across_top, up_top = 0, BASES // 2 * cols
    gather_top = up_top + 3 * rows
    vertical = tables[pl.ds(up_top, 3 * rows), pl.ds(0, rows + 2 * TILE)]

    def across(c):
        return tables[pl.ds(across_top + c * cols, cols), pl.ds(0, cols)]

    one_hot = (position == iota((LANES, pieces), 0)).astype(F32).astype(BF16)
    e_rows = jnp.right_shift(iota((span, LANES), 0), 4) == iota((span, LANES), 1)
    e_rows = e_rows.astype(F32).astype(BF16)
    row_hot = nt(e_rows[:, :pieces], one_hot)
    piece_hot = nt((iota((TILE, pieces), 0) == iota((TILE, pieces), 1)).astype(F32).astype(BF16), one_hot)

    def member(d, hot):
        chosen_one = jnp.where(iota(hot.shape, 1) == slots[d], hot, 0.0)
        return jnp.sum(chosen_one, axis=1, keepdims=True)

    def summed(values):
        return jnp.sum(values.reshape(pieces, TILE, values.shape[1]), axis=1)

    def keep(width):
        return (iota((span, width), 0) & (TILE - 1)) == (iota((span, width), 1) & (TILE - 1))

    wide_n = len(pairs) * TILE
    wide_b = BASES * TILE
    normal = jnp.zeros((pieces, wide_n), F32)
    right = jnp.zeros((pieces, wide_b), F32)
    for d in range(distinct):
        for h in range(halves):
            @pl.when(me != lead + h)
            def _():
                template_copy(h, me, d).wait_recv()

            pl.when(above)(edge_copy(0, h, me, d).wait_recv)
            pl.when(below)(edge_copy(1, h, me, d).wait_recv)
        template = jnp.concatenate([template_v[d, h] for h in range(halves)], axis=1)
        smooth = nn(vertical, template).astype(BF16)
        planes = [None] * BASES
        for c in range(3):
            taken = [a for a in range(BASES) if basis_cols[a] == c]
            product = nn(smooth[: len(taken) * rows], across(c)).astype(BF16)
            for a in taken:
                r = basis_rows[a]
                planes[a] = product[r * rows : (r + 1) * rows]
        for a in range(BASES):
            for t in range(blocks):
                basis[d, pl.ds(a * TILE, TILE), pl.ds(t * cols, cols)] = planes[a][
                    t * TILE : (t + 1) * TILE
                ]
        for n, (a, c) in enumerate(pairs):
            product = planes[a] * planes[c]
            for t in range(blocks):
                prods[d, pl.ds(n * TILE, TILE), pl.ds(t * cols, cols)] = product[
                    t * TILE : (t + 1) * TILE
                ]
        belongs = member(d, row_hot)
        normal = normal + summed(jnp.where(keep(wide_n), nt(use[...], prods[d]), 0.0) * belongs)
        right = right + summed(jnp.where(keep(wide_b), nt(use_image[...], basis[d]), 0.0) * belongs)

    gather_n = tables[pl.ds(gather_top, wide_n), pl.ds(0, LANES)]
    gather_b = tables[pl.ds(gather_top + wide_n, wide_b), pl.ds(0, LANES)]
    system = nn(thirds(normal), gather_n) + nn(thirds(right), gather_b)
    small[...] = sum(system[k * pieces : (k + 1) * pieces] for k in range(3))
    exchanges = []
    for hop in range(1, strips):
        exchanges.append(pltpu.make_async_remote_copy(
            src_ref=small, dst_ref=small_in.at[hop - 1],
            send_sem=st_send.at[hop - 1], recv_sem=st_recv.at[hop - 1],
            device_id={"strip": lax.rem(strip + hop, strips)}, device_id_type=MESH,
        ))
    for copy in exchanges:
        copy.start()

    wide_c = 2 * wide_b
    column = iota((16, wide_c), 1)
    source = jnp.where(
        column < wide_b, jnp.right_shift(column, 4), jnp.right_shift(column - wide_b, 4) + 8
    )
    e3 = (source == iota((16, wide_c), 0)).astype(F32).astype(BF16)
    diagonal = iota((TILE, wide_c), 0) == (iota((TILE, wide_c), 1) & (TILE - 1))
    belongs = [member(d, piece_hot) for d in range(distinct)]

    for h in range(halves):
        @pl.when(me != lead + h)
        def _():
            owned_copy(h, me).wait_recv()

        coadd_out[:, pl.ds(h * LANES, LANES)] = owned[h]

    full = small[...]
    for hop in range(1, strips):
        exchanges[hop - 1].wait_recv()
        full = full + small_in[hop - 1]
    full = jnp.transpose(full)

    line = iota((8, pieces), 0)
    table = [
        full[a * 8 : (a + 1) * 8] + jnp.where(line == a, 1.0, 0.0) for a in range(BASES)
    ]
    for column in range(BASES):
        pivot = table[column] / table[column][column : column + 1]
        for i in range(BASES):
            if i != column:
                table[i] = table[i] - table[i][column : column + 1] * pivot
        table[column] = pivot
    found = jnp.zeros((8, pieces), F32)
    for a in range(BASES):
        found = found + jnp.where(line == a, table[a][BASES : BASES + 1], 0.0)
    high = found.astype(BF16).astype(F32)
    low = found - high
    both = jnp.concatenate([high, low], axis=0).astype(BF16)
    spread = tn(both, e3)
    for d in range(distinct):
        part = spread * belongs[d]
        for j in range(pieces):
            mixers[d, pl.ds(j * TILE, TILE), :] = jnp.where(
                diagonal, part[j : j + 1], 0.0
            ).astype(BF16)

    for copy in exchanges:
        copy.wait_send()
    for h in range(halves):
        @pl.when(me != lead + h)
        def _():
            for copy in sum_copies(h, me):
                copy.wait_send()

    @pl.when(owning)
    def _():
        def sent(v):
            for d in range(distinct):
                pl.when(below)(edge_copy(0, mine, v, d).wait_send)
                pl.when(above)(edge_copy(1, mine, v, d).wait_send)

            @pl.when(me != v)
            def _():
                for d in range(distinct):
                    template_copy(mine, v, d).wait_send()
                owned_copy(mine, v).wait_send()

        each(visits, sent)


def finish(coadd_in, image_v, basis, mixers, coadd_out, diff_out, diff_v, out_sem):
    distinct = basis.shape[0]
    blocks, pieces, _, cols = image_v.shape
    span = pieces * TILE
    stores = [pltpu.make_async_copy(coadd_in, coadd_out.at[0, 0], out_sem.at[0])]
    stores[0].start()
    for t in range(blocks):
        lanes = pl.ds(t * cols, cols)
        fitted = jnp.zeros((span, cols), F32)
        for d in range(distinct):
            planes = basis[d, :, lanes]
            fitted = fitted + nn(mixers[d], jnp.concatenate([planes, planes], axis=0))
        result = (image_v[t].reshape(span, cols).astype(F32) - fitted).astype(BF16)
        diff_v[t] = result.reshape(pieces, TILE, cols)
        copy = pltpu.make_async_copy(
            diff_v.at[t], diff_out.at[0, :, pl.ds(t * TILE, TILE), :], out_sem.at[1 + t]
        )
        copy.start()
        stores.append(copy)
    for copy in stores:
        copy.wait()


def body(visits, strips, images, mask_bits, visit_weight, intersection, patch_owner):
    _, pieces, rows, cols = images.shape
    blocks = rows // TILE
    halves = cols // LANES
    distinct = max(1, patch_owner.shape[0] // 2)
    span = pieces * TILE
    taps = kernel_taps()
    width = -(-max(LANES, cols, rows + 2 * TILE) // LANES) * LANES
    tables = jnp.asarray(np.concatenate([
        np.pad(part, ((0, 0), (0, width - part.shape[1])))
        for part in (
            np.transpose(band_matrix(taps, cols, cols, HALF), (0, 2, 1)).reshape(3 * cols, cols),
            band_matrix(taps, rows, rows + 2 * TILE, HALF - TILE).reshape(3 * rows, -1),
            gather_matrix(),
        )
    ]), BF16)
    hbm = pl.BlockSpec(memory_space=pltpu.HBM)
    vmem = pl.BlockSpec(memory_space=pltpu.VMEM)
    dma = pltpu.SemaphoreType.DMA
    cross = intersection.reshape(1, pieces)
    others = max(1, strips - 1)
    middle = pl.pallas_call(
        functools.partial(kernel, visits, strips, distinct),
        out_shape=(
            jax.ShapeDtypeStruct((rows, cols), BF16),
            jax.ShapeDtypeStruct((blocks, pieces, TILE, cols), BF16),
            jax.ShapeDtypeStruct((distinct, BASES * TILE, blocks * cols), BF16),
            jax.ShapeDtypeStruct((distinct, span, 2 * BASES * TILE), BF16),
        ),
        in_specs=[hbm, hbm, hbm, hbm, hbm, hbm],
        out_specs=(vmem, vmem, vmem, vmem),
        scratch_shapes=[
            pltpu.VMEM((blocks, pieces, TILE, cols), jnp.int32),
            pltpu.VMEM(tables.shape, BF16),
            pltpu.VMEM((1, pieces), BF16),
            pltpu.VMEM((1, pieces), jnp.int32),
            pltpu.SMEM((1, pieces), jnp.int32),
            pltpu.SMEM(patch_owner.shape, jnp.int32),
            pltpu.VMEM((span, blocks * cols), BF16),
            pltpu.VMEM((span, blocks * cols), BF16),
            pltpu.VMEM((halves, distinct, 2, rows, LANES), BF16),
            pltpu.VMEM((visits, distinct, 2, rows, LANES), BF16),
            pltpu.VMEM((1, LANES), F32),
            pltpu.VMEM((visits, 1, LANES), F32),
            pltpu.VMEM((visits, rows, LANES), BF16),
            pltpu.VMEM((visits, distinct, rows, LANES), BF16),
            pltpu.VMEM((distinct, halves, rows + 2 * TILE, LANES), BF16),
            pltpu.VMEM((halves, rows, LANES), BF16),
            pltpu.VMEM((distinct, len(pairs) * TILE, blocks * cols), BF16),
            pltpu.VMEM((pieces, LANES), F32),
            pltpu.VMEM((others, pieces, LANES), F32),
            dma((2, blocks)),
            dma,
            dma((4,)),
            dma((halves,)),
            dma((visits,)),
            dma((halves,)),
            dma((visits,)),
            dma((visits, distinct)),
            dma((halves, distinct)),
            dma((2, visits, distinct)),
            dma((2, halves, distinct)),
            dma((visits,)),
            dma((halves,)),
            dma((others,)),
            dma((others,)),
        ],
        compiler_params=pltpu.CompilerParams(
            collective_id=0, has_side_effects=True, vmem_limit_bytes=55_100_000
        ),
        name="coadd_solve",
    )(images, mask_bits, visit_weight, cross, patch_owner, tables)
    return pl.pallas_call(
        finish,
        out_shape=(
            jax.ShapeDtypeStruct((1, 1, rows, cols), BF16),
            jax.ShapeDtypeStruct(images.shape, BF16),
        ),
        in_specs=[vmem, vmem, vmem, vmem],
        out_specs=(hbm, hbm),
        scratch_shapes=[
            pltpu.VMEM((blocks, pieces, TILE, cols), BF16),
            dma((1 + blocks,)),
        ],
        compiler_params=pltpu.CompilerParams(vmem_limit_bytes=40 * 1024 * 1024),
        name="difference",
    )(*middle)


def solution(mesh):
    in_specs = (
        P("band", ("groups", "visit"), "strip", None),
        P("band", ("groups", "visit"), "strip", None),
        P("band", ("groups", "visit")),
        P(("groups", "visit"), None),
        P("groups"),
    )
    out_specs = (
        P("band", ("groups", "visit"), "strip", None),
        P("band", ("groups", "visit"), "strip", None),
    )
    step = functools.partial(body, mesh.shape["visit"], mesh.shape["strip"])
    return jax.shard_map(step, mesh=mesh, in_specs=in_specs, out_specs=out_specs, check_vma=False)
```

```python
import functools

import jax
import jax.numpy as jnp
import numpy as np
from jax import lax
from jax.experimental import pallas as pl
from jax.experimental.pallas import tpu as pltpu
from jax.sharding import PartitionSpec as P

BASES = 6
HALF = 9
TILE = 16
LANES = 128

basis_rows = (0, 0, 1, 0, 2, 1)
basis_cols = (0, 1, 0, 2, 0, 1)
pairs = tuple((a, c) for a in range(BASES) for c in range(a, BASES))
MESH = pl.DeviceIdType.MESH
F32 = jnp.float32
BF16 = jnp.bfloat16


def kernel_taps():
    offsets = np.arange(2 * HALF + 1).astype(np.float32) - HALF
    gaussian = np.exp(-offsets * offsets / np.float32(18.0))
    centre = np.sum(offsets * offsets * gaussian * gaussian) / np.sum(gaussian * gaussian)
    table = np.stack([gaussian, offsets * gaussian, (offsets * offsets - centre) * gaussian])
    table = table / np.sqrt(np.sum(table * table, axis=1, keepdims=True))
    return table.astype(BF16).astype(np.float32)


def band_matrix(table, lead, trail, displace):
    index = np.arange(trail)[None, :] - np.arange(lead)[:, None] + displace
    inside = (index >= 0) & (index <= 2 * HALF)
    return np.where(inside[None], table[:, np.clip(index, 0, 2 * HALF)], 0.0)


def iota(shape, dim):
    return lax.broadcasted_iota(jnp.int32, shape, dim)


def nn(a, b):
    return jnp.dot(a, b, preferred_element_type=F32)


def nt(a, b):
    return lax.dot_general(a, b, (((1,), (1,)), ((), ())), preferred_element_type=F32)


def tn(a, b):
    return lax.dot_general(a, b, (((0,), (0,)), ((), ())), preferred_element_type=F32)


def each(count, step):
    if count <= 4:
        for k in range(count):
            step(k)
    else:
        def body(k, carry):
            step(k)
            return carry

        lax.fori_loop(0, count, body, 0)


def thirds(value):
    high = value.astype(BF16)
    rest = value - high.astype(F32)
    middle = rest.astype(BF16)
    low = (rest - middle.astype(F32)).astype(BF16)
    return jnp.concatenate([high, middle, low], axis=0)


def kernel(
    visits, strips, bands, distinct,
    images, masks, weight_in, cross_in, owner_in, table_in,
    coadd_out, image_s, basis, mixers, order_out,
    mask_v, image_v, tables, weight, cross, owner, use, use_image, turned, turned_image, send, recv,
    patches, chosen, template_v, owned, prods, small, small_in,
    first_sem, in_sem, const_sem, sum_send, sum_recv, template_send, template_recv, owned_recv,
    st_send, st_recv,
):
    pieces, rows, cols = images.shape[1:]
    blocks = rows // TILE
    chunk = rows // in_sem.shape[1]
    span = pieces * TILE
    cap = pieces // distinct
    halves = cols // LANES
    lead = (visits - halves) // 2
    last = bands - 1
    sheet = distinct * 2 * rows
    parcel = sheet + TILE
    me = lax.axis_index("visit")
    strip = lax.axis_index("strip")
    band = lax.axis_index("band")
    above = strip > 0
    below = strip < strips - 1
    mine = me - lead
    central = (me >= lead) & (me < lead + halves)
    owning = central & (band == last)
    reach = 1 + above.astype(jnp.int32) + below.astype(jnp.int32)

    firsts = [
        pltpu.make_async_copy(cross_in, cross, first_sem.at[0]),
        pltpu.make_async_copy(owner_in, owner, first_sem.at[1]),
        pltpu.make_async_copy(weight_in, weight, first_sem.at[2]),
    ]
    for copy in firsts:
        copy.start()

    barrier = pltpu.get_barrier_semaphore()

    def greet(v, hop, b):
        target = {"visit": v, "strip": lax.rem(strip + hop, strips), "band": b}
        pl.semaphore_signal(barrier, inc=1, device_id=target, device_id_type=MESH)

    def near(hop, step):
        if hop == 0:
            step()
        elif hop == 1 and strips == 2:
            step()
        elif hop == 1:
            pl.when(below)(step)
        elif hop == strips - 1:
            pl.when(above)(step)

    def adjoining(hop):
        if hop in (0, 1) and strips == 2:
            return jnp.bool_(True)
        return below if hop == 1 else (above if hop == strips - 1 else jnp.bool_(False))

    @pl.when(owning)
    def _():
        for hop in sorted({0, 1 % strips, strips - 1}):
            def greet_strip():
                def greet_visit(v):
                    for b in range(bands):
                        if hop == 0 and b == last:
                            pl.when(me != v)(functools.partial(greet, v, hop, b))
                        else:
                            greet(v, hop, b)

                each(visits, greet_visit)

            near(hop, greet_strip)
        for hop in range(2, strips - 1):
            greet(me, hop, band)
        for hop in sorted({1 % strips, strips - 1} - {0}):
            if strips > 2:
                pl.when(jnp.logical_not(adjoining(hop)))(functools.partial(greet, me, hop, band))

    @pl.when(jnp.logical_not(owning))
    def _():
        for hop in sorted({0, 1 % strips, strips - 1}):
            def greet_owners():
                for h in range(halves):
                    greet(lead + h, hop, last)

            near(hop, greet_owners)
        for hop in range(1, strips):
            greet(me, hop, band)

    loads = []
    for k in range(rows // chunk):
        part = pl.ds(k * chunk, chunk)
        loads.append((
            pltpu.make_async_copy(masks.at[0, :, part, :], mask_v.at[:, part, :], in_sem.at[0, k]),
            pltpu.make_async_copy(images.at[0, :, part, :], image_v.at[:, part, :], in_sem.at[1, k]),
        ))
        for copy in loads[k]:
            copy.start()
    constants = pltpu.make_async_copy(table_in, tables, const_sem)
    constants.start()

    for copy in firsts:
        copy.wait()
    seats = [owner[cross[0, j]] for j in range(pieces)]
    slots = [jnp.int32(0)] * distinct
    rank = jnp.int32(0)
    for q in range(visits):
        present = jnp.int32(0)
        for j in range(pieces):
            present = present | jnp.where(seats[j] == q, 1, 0)
        for d in range(distinct):
            slots[d] = slots[d] + jnp.where((present == 1) & (rank == d), q, 0)
        rank = rank + present

    position = jnp.zeros((1, pieces), jnp.int32)
    for j in range(pieces):
        position = position + jnp.where(iota((1, pieces), 1) == j, seats[j], 0)
    e2 = iota((pieces, span), 0) == jnp.right_shift(iota((pieces, span), 1), 4)
    e2 = e2.astype(F32).astype(BF16)
    pair = jnp.where(
        iota((8, pieces), 0) == 0, weight[...].astype(F32), position.astype(F32)
    ).astype(BF16)
    wide = nn(pair, e2)
    same = (iota((TILE, span), 0) & (TILE - 1)) == (iota((TILE, span), 1) & (TILE - 1))
    adder = jnp.concatenate([
        jnp.where(same & (wide[1:2] == lax.convert_element_type(slots[d], F32)), wide[0:1], 0.0)
        for d in range(distinct)
    ], axis=0).astype(BF16)
    names = jnp.zeros((TILE, LANES), jnp.int32)
    for d in range(distinct):
        names = names + jnp.where(iota((TILE, LANES), 0) == d, slots[d], 0)
    for h in range(halves):
        send[h, pl.ds(sheet, TILE), :] = names.astype(F32).astype(BF16)

    for t in range(blocks):
        if t * TILE % chunk == 0:
            for copy in loads[t * TILE // chunk]:
                copy.wait()
        piece_rows = pl.ds(t * TILE, TILE)
        lanes = pl.ds(t * cols, cols)
        usable = ((mask_v[:, piece_rows, :].reshape(span, cols) & 3) != 3).astype(F32).astype(BF16)
        masked = usable * image_v[:, piece_rows, :].reshape(span, cols)
        use[:, :, lanes] = usable.reshape(pieces, TILE, cols)
        use_image[:, :, lanes] = masked.reshape(pieces, TILE, cols)
        for part, value in enumerate((masked, usable)):
            total = nn(adder, value).astype(BF16)
            for d in range(distinct):
                for h in range(halves):
                    send[h, pl.ds((d * 2 + part) * rows + t * TILE, TILE), :] = total[
                        d * TILE : (d + 1) * TILE, h * LANES : (h + 1) * LANES
                    ]

    def parcel_at(b, v):
        return pl.multiple_of((b * visits + v) * parcel, TILE)

    def some(count):
        return recv.at[pl.ds(0, count), :]

    def sum_copy(h, b):
        return pltpu.make_async_remote_copy(
            src_ref=send.at[h], dst_ref=recv.at[pl.ds(parcel_at(b, me), parcel), :],
            send_sem=sum_send, recv_sem=sum_recv.at[b],
            device_id={"visit": lead + h, "band": last}, device_id_type=MESH,
        )

    def template_copy(b, h, v, d):
        return pltpu.make_async_remote_copy(
            src_ref=chosen.at[b, v, d], dst_ref=template_v.at[d, h, pl.ds(TILE, rows), :],
            send_sem=template_send, recv_sem=template_recv.at[d],
            device_id={"visit": v, "band": b}, device_id_type=MESH,
        )

    def edge_copy(way, b, h, v, d):
        step, source, target = ((1, rows - TILE, 0), (strips - 1, 0, rows + TILE))[way]
        return pltpu.make_async_remote_copy(
            src_ref=chosen.at[b, v, d, pl.ds(source, TILE), :],
            dst_ref=template_v.at[d, h, pl.ds(target, TILE), :],
            send_sem=template_send, recv_sem=template_recv.at[d],
            device_id={"visit": v, "strip": lax.rem(strip + step, strips), "band": b},
            device_id_type=MESH,
        )

    def owned_copy(b, h, v):
        return pltpu.make_async_remote_copy(
            src_ref=patches.at[b, v], dst_ref=owned.at[h],
            send_sem=template_send, recv_sem=owned_recv,
            device_id={"visit": v, "band": b}, device_id_type=MESH,
        )

    def wait_for(sem, count):
        pltpu.make_async_copy(some(count), some(count), sem).wait()

    met = jnp.where(
        owning, visits * bands * reach - 1 + strips - reach, halves * reach + strips - 1
    )
    pl.semaphore_wait(barrier, met)
    for b in range(bands):
        for h in range(halves):
            @pl.when((band == b) & jnp.logical_not(owning & (mine == h)))
            def _():
                sum_copy(h, b).start()

    @pl.when(jnp.logical_not(above))
    def _():
        template_v[:, :, pl.ds(0, TILE), :] = jnp.zeros((distinct, halves, TILE, LANES), BF16)

    @pl.when(jnp.logical_not(below))
    def _():
        template_v[:, :, pl.ds(rows + TILE, TILE), :] = jnp.zeros(
            (distinct, halves, TILE, LANES), BF16
        )

    def reduce(b):
        if b == last:
            recv[pl.ds(parcel_at(b, me), parcel), :] = send[mine]
        wait_for(sum_recv.at[b], (visits if b != last else visits - 1) * parcel)

        def id_tile(v, d):
            names = recv[pl.ds(parcel_at(b, v) + sheet, TILE), :].astype(F32)
            return jnp.broadcast_to(names[d : d + 1], (TILE, LANES))

        def value(v, d, part, t):
            start = pl.multiple_of(parcel_at(b, v) + (d * 2 + part) * rows + t * TILE, TILE)
            return recv[pl.ds(start, TILE), :].astype(F32)

        def one_tile(t):
            piece_rows = pl.ds(t * TILE, TILE)
            if visits <= 4:
                tiles = [[id_tile(v, d) for d in range(distinct)] for v in range(visits)]
                finals = []
                for q in range(visits):
                    numerator = jnp.zeros((TILE, LANES), F32)
                    denominator = jnp.zeros((TILE, LANES), F32)
                    for v in range(visits):
                        for d in range(distinct):
                            here = tiles[v][d] == float(q)
                            numerator += jnp.where(here, value(v, d, 0, t), 0.0)
                            denominator += jnp.where(here, value(v, d, 1, t), 0.0)
                    final = numerator / jnp.maximum(denominator, 1.0)
                    patches[b, q, piece_rows, :] = final.astype(BF16)
                    finals.append(final)
                for v in range(visits):
                    for d in range(distinct):
                        picked = finals[0]
                        for q in range(1, visits):
                            picked = jnp.where(tiles[v][d] == float(q), finals[q], picked)
                        chosen[b, v, d, piece_rows, :] = picked.astype(BF16)
                return

            def one_patch(q):
                number = lax.convert_element_type(q, F32)

                def add(v, carry):
                    numerator, denominator = carry
                    for d in range(distinct):
                        here = id_tile(v, d) == number
                        numerator += jnp.where(here, value(v, d, 0, t), 0.0)
                        denominator += jnp.where(here, value(v, d, 1, t), 0.0)
                    return numerator, denominator

                zero = jnp.zeros((TILE, LANES), F32)
                numerator, denominator = lax.fori_loop(0, visits, add, (zero, zero))
                final = numerator / jnp.maximum(denominator, 1.0)
                patches[b, q, piece_rows, :] = final.astype(BF16)

            def pick(v):
                for d in range(distinct):
                    tile = id_tile(v, d)

                    def better(q, picked):
                        final = patches[b, q, piece_rows, :].astype(F32)
                        return jnp.where(tile == lax.convert_element_type(q, F32), final, picked)

                    picked = lax.fori_loop(0, visits, better, jnp.zeros((TILE, LANES), F32))
                    chosen[b, v, d, piece_rows, :] = picked.astype(BF16)

            each(visits, one_patch)
            each(visits, pick)

        for t in range(blocks):
            one_tile(t)

        for d in range(distinct):
            def templates(v):
                pl.when(below)(edge_copy(0, b, mine, v, d).start)
                pl.when(above)(edge_copy(1, b, mine, v, d).start)
                if b == last:
                    pl.when(me != v)(template_copy(b, mine, v, d).start)
                else:
                    template_copy(b, mine, v, d).start()

            each(visits, templates)
        if b == last:
            template_v[:, mine, pl.ds(TILE, rows), :] = chosen[b, me]

    @pl.when(owning)
    def _():
        for b in range(bands):
            reduce(b)

        def owners(v):
            for b in range(bands):
                if b == last:
                    pl.when(me != v)(owned_copy(b, mine, v).start)
                else:
                    owned_copy(b, mine, v).start()

        each(visits, owners)
        owned[mine] = patches[last, me]

    places = []
    for d in range(distinct):
        count = jnp.int32(0)
        found = [jnp.int32(0)] * cap
        for j in range(pieces):
            hit = seats[j] == slots[d]
            for k in range(cap):
                found[k] = found[k] + jnp.where(hit & (count == k), j, 0)
            count = count + jnp.where(hit, 1, 0)
        places += found
    order = jnp.zeros((1, LANES), jnp.int32)
    for k in range(pieces):
        order = order + jnp.where(iota((1, LANES), 1) == k, places[k], 0)
        for t in range(blocks):
            image_s[t, k] = image_v[places[k], pl.ds(t * TILE, TILE), :]
    order_out[...] = order
    for d in range(distinct):
        for t in range(blocks):
            lanes = pl.ds(t * cols, cols)
            for source, target in ((use, turned), (use_image, turned_image)):
                stack = [source[places[d * cap + k], :, lanes] for k in range(cap)]
                target[d, lanes, :] = jnp.transpose(jnp.concatenate(stack, axis=0))
    constants.wait()

    up_top = BASES // 2 * cols
    vertical = tables[pl.ds(up_top, 3 * rows), pl.ds(0, rows + 2 * TILE)]

    def across(c):
        return tables[pl.ds(c * cols, cols), pl.ds(0, cols)]

    wide_n = len(pairs) * TILE
    wide_b = BASES * TILE
    lines = small.shape[0]

    def kept(values):
        keep = (iota(values.shape, 0) & (TILE - 1)) == (iota(values.shape, 1) & (TILE - 1))
        return jnp.where(keep, values, 0.0)

    system = jnp.zeros((lines, LANES), F32)
    for d in range(distinct):
        for local in (False, True):
            for sides in range(3 if strips > 2 else 2):
                count = (halves - local) * rows + halves * sides * TILE

                @pl.when((owning == local) & (reach == sides + 1))
                def _():
                    if count:
                        wait_for(template_recv.at[d], count)

        template = jnp.concatenate([template_v[d, h] for h in range(halves)], axis=1)
        smooth = nn(vertical, template).astype(BF16)
        planes = [None] * BASES
        for c in range(3):
            taken = [a for a in range(BASES) if basis_cols[a] == c]
            product = nn(smooth[: len(taken) * rows], across(c)).astype(BF16)
            for a in taken:
                r = basis_rows[a]
                planes[a] = product[r * rows : (r + 1) * rows]
        for a in range(BASES):
            for t in range(blocks):
                basis[d, pl.ds(a * TILE, TILE), pl.ds(t * cols, cols)] = planes[a][
                    t * TILE : (t + 1) * TILE
                ]
        for n, (a, c) in enumerate(pairs):
            product = planes[a] * planes[c]
            for t in range(blocks):
                prods[pl.ds(n * TILE, TILE), pl.ds(t * cols, cols)] = product[
                    t * TILE : (t + 1) * TILE
                ]
        sums = jnp.concatenate([
            kept(nn(prods[...], turned[d])),
            kept(nn(basis[d], turned_image[d])),
            jnp.zeros((lines * TILE - wide_n - wide_b, cap * TILE), F32),
        ], axis=0)
        sums = jnp.sum(sums.reshape(lines, TILE, cap * TILE), axis=1)
        collect = jnp.right_shift(iota((cap * TILE, LANES), 0), 4) + d * cap
        collect = (collect == iota((cap * TILE, LANES), 1)).astype(F32).astype(BF16)
        gathered = nn(thirds(sums), collect)
        system = system + sum(gathered[k * lines : (k + 1) * lines] for k in range(3))
    small[...] = system
    exchanges = []
    for hop in range(1, strips):
        exchanges.append(pltpu.make_async_remote_copy(
            src_ref=small, dst_ref=small_in.at[hop - 1],
            send_sem=st_send, recv_sem=st_recv,
            device_id={"strip": lax.rem(strip + hop, strips)}, device_id_type=MESH,
        ))
    for copy in exchanges:
        copy.start()

    wide_c = 2 * wide_b
    column = iota((16, wide_c), 1)
    source = jnp.where(
        column < wide_b, jnp.right_shift(column, 4), jnp.right_shift(column - wide_b, 4) + 8
    )
    e3 = (source == iota((16, wide_c), 0)).astype(F32).astype(BF16)
    diagonal = iota((TILE, wide_c), 0) == (iota((TILE, wide_c), 1) & (TILE - 1))

    for local in (False, True):
        @pl.when(owning == local)
        def _():
            if halves - local:
                wait_for(owned_recv, (halves - local) * rows)
    for h in range(halves):
        coadd_out[:, pl.ds(h * LANES, LANES)] = owned[h]

    if exchanges:
        pltpu.make_async_copy(small_in, small_in, st_recv).wait()

    def line_of(n):
        value = small[pl.ds(n, 1), :]
        for hop in range(1, strips):
            value = value + small_in[hop - 1, pl.ds(n, 1), :]
        return value

    entry = {pairs[n]: line_of(n) + float(pairs[n][0] == pairs[n][1]) for n in range(len(pairs))}
    side = [line_of(len(pairs) + a) for a in range(BASES)]
    inverse = [None] * BASES
    for k in range(BASES):
        inverse[k] = 1.0 / entry[k, k]
        for i in range(k + 1, BASES):
            factor = entry[k, i] * inverse[k]
            for c in range(i, BASES):
                entry[i, c] = entry[i, c] - factor * entry[k, c]
            side[i] = side[i] - factor * side[k]
    for k in reversed(range(BASES)):
        for c in range(k + 1, BASES):
            side[k] = side[k] - entry[k, c] * side[c]
        side[k] = side[k] * inverse[k]
    found = jnp.zeros((8, LANES), F32)
    for a in range(BASES):
        found = found + jnp.where(iota((8, LANES), 0) == a, side[a], 0.0)
    high = found.astype(BF16).astype(F32)
    low = found - high
    both = jnp.concatenate([high, low], axis=0)[:, :pieces].astype(BF16)
    spread = tn(both, e3)
    for k in range(pieces):
        mixers[k // cap, pl.ds(k % cap * TILE, TILE), :] = jnp.where(
            diagonal, spread[k : k + 1], 0.0
        ).astype(BF16)

    for copy in exchanges:
        copy.wait_send()
    for local in (False, True):
        @pl.when(owning == local)
        def _():
            if halves - local:
                wait_for(sum_send, (halves - local) * parcel)
    for sides in range(3 if strips > 2 else 2):
        mains = (bands * visits - 1) * (distinct + 1) * rows
        edges = bands * visits * distinct * sides * TILE

        @pl.when(owning & (reach == sides + 1))
        def _():
            wait_for(template_send, mains + edges)


def finish(coadd_in, image_s, basis, mixers, order, coadd_out, diff_out, diff_v, places, out_sem):
    distinct = basis.shape[0]
    blocks, pieces, _, cols = image_s.shape
    cap = pieces // distinct
    bring = pltpu.make_async_copy(order, places, out_sem.at[1 + blocks])
    bring.start()
    stores = [pltpu.make_async_copy(coadd_in, coadd_out.at[0, 0], out_sem.at[0])]
    stores[0].start()
    bring.wait()
    for t in range(blocks):
        lanes = pl.ds(t * cols, cols)
        for d in range(distinct):
            planes = basis[d, :, lanes]
            fitted = nn(mixers[d], jnp.concatenate([planes, planes], axis=0))
            for k in range(cap):
                value = image_s[t, d * cap + k].astype(F32) - fitted[k * TILE : (k + 1) * TILE]
                diff_v[t, places[0, d * cap + k]] = value.astype(BF16)
        copy = pltpu.make_async_copy(
            diff_v.at[t], diff_out.at[0, :, pl.ds(t * TILE, TILE), :], out_sem.at[1 + t]
        )
        copy.start()
        stores.append(copy)
    for copy in stores:
        copy.wait()


def body(visits, strips, bands, images, mask_bits, visit_weight, intersection, patch_owner):
    _, pieces, rows, cols = images.shape
    blocks = rows // TILE
    halves = cols // LANES
    distinct = max(1, patch_owner.shape[0] // 2)
    cap = pieces // distinct
    taps = kernel_taps()
    width = -(-max(LANES, cols, rows + 2 * TILE) // LANES) * LANES
    tables = jnp.asarray(np.concatenate([
        np.pad(part, ((0, 0), (0, width - part.shape[1])))
        for part in (
            np.transpose(band_matrix(taps, cols, cols, HALF), (0, 2, 1)).reshape(3 * cols, cols),
            band_matrix(taps, rows, rows + 2 * TILE, HALF - TILE).reshape(3 * rows, -1),
        )
    ]), BF16)
    hbm = pl.BlockSpec(memory_space=pltpu.HBM)
    vmem = pl.BlockSpec(memory_space=pltpu.VMEM)
    dma = pltpu.SemaphoreType.DMA
    cross = intersection.reshape(1, pieces)
    others = max(1, strips - 1)
    parcel = distinct * 2 * rows + TILE
    lines = -(-(len(pairs) + BASES) // 8) * 8
    middle = pl.pallas_call(
        functools.partial(kernel, visits, strips, bands, distinct),
        out_shape=(
            jax.ShapeDtypeStruct((rows, cols), BF16),
            jax.ShapeDtypeStruct((blocks, pieces, TILE, cols), BF16),
            jax.ShapeDtypeStruct((distinct, BASES * TILE, blocks * cols), BF16),
            jax.ShapeDtypeStruct((distinct, cap * TILE, 2 * BASES * TILE), BF16),
            jax.ShapeDtypeStruct((1, LANES), jnp.int32),
        ),
        in_specs=[hbm, hbm, hbm, hbm, hbm, hbm],
        out_specs=(vmem, vmem, vmem, vmem, vmem),
        scratch_shapes=[
            pltpu.VMEM((pieces, rows, cols), jnp.int32),
            pltpu.VMEM((pieces, rows, cols), BF16),
            pltpu.VMEM(tables.shape, BF16),
            pltpu.VMEM((1, pieces), BF16),
            pltpu.SMEM((1, pieces), jnp.int32),
            pltpu.SMEM(patch_owner.shape, jnp.int32),
            pltpu.VMEM((pieces, TILE, blocks * cols), BF16),
            pltpu.VMEM((pieces, TILE, blocks * cols), BF16),
            pltpu.VMEM((distinct, blocks * cols, cap * TILE), BF16),
            pltpu.VMEM((distinct, blocks * cols, cap * TILE), BF16),
            pltpu.VMEM((halves, parcel, LANES), BF16),
            pltpu.VMEM((bands * visits * parcel, LANES), BF16),
            pltpu.VMEM((bands, visits, rows, LANES), BF16),
            pltpu.VMEM((bands, visits, distinct, rows, LANES), BF16),
            pltpu.VMEM((distinct, halves, rows + 2 * TILE, LANES), BF16),
            pltpu.VMEM((halves, rows, LANES), BF16),
            pltpu.VMEM((len(pairs) * TILE, blocks * cols), BF16),
            pltpu.VMEM((lines, LANES), F32),
            pltpu.VMEM((others, lines, LANES), F32),
            dma((3,)),
            dma((2, 2)),
            dma,
            dma,
            dma((bands,)),
            dma,
            dma((distinct,)),
            dma,
            dma,
            dma,
        ],
        compiler_params=pltpu.CompilerParams(
            collective_id=0, has_side_effects=True, vmem_limit_bytes=40_000_000
        ),
        name="coadd_solve",
    )(*(
        pltpu.with_memory_space_constraint(part, pltpu.HBM)
        for part in (images, mask_bits, visit_weight, cross, patch_owner, tables)
    ))
    return pl.pallas_call(
        finish,
        out_shape=(
            jax.ShapeDtypeStruct((1, 1, rows, cols), BF16),
            jax.ShapeDtypeStruct(images.shape, BF16),
        ),
        in_specs=[vmem, vmem, vmem, vmem, vmem],
        out_specs=(hbm, hbm),
        scratch_shapes=[
            pltpu.VMEM((blocks, pieces, TILE, cols), BF16),
            pltpu.SMEM((1, LANES), jnp.int32),
            dma((2 + blocks,)),
        ],
        compiler_params=pltpu.CompilerParams(vmem_limit_bytes=40 * 1024 * 1024),
        name="difference",
    )(*middle)


def solution(mesh):
    in_specs = (
        P("band", ("groups", "visit"), "strip", None),
        P("band", ("groups", "visit"), "strip", None),
        P("band", ("groups", "visit")),
        P(("groups", "visit"), None),
        P("groups"),
    )
    out_specs = (
        P("band", ("groups", "visit"), "strip", None),
        P("band", ("groups", "visit"), "strip", None),
    )
    step = functools.partial(
        body, mesh.shape["visit"], mesh.shape["strip"], mesh.shape["band"]
    )
    return jax.shard_map(step, mesh=mesh, in_specs=in_specs, out_specs=out_specs, check_vma=False)
```

```python
import functools

import jax
import jax.numpy as jnp
import numpy as np
from jax import lax
from jax.experimental import pallas as pl
from jax.experimental.pallas import tpu as pltpu
from jax.sharding import PartitionSpec as P

BASES = 6
HALF = 9
TILE = 16
LANES = 128

basis_rows = (0, 0, 1, 0, 2, 1)
basis_cols = (0, 1, 0, 2, 0, 1)
pairs = tuple((a, c) for a in range(BASES) for c in range(a, BASES))
MESH = pl.DeviceIdType.MESH
F32 = jnp.float32
BF16 = jnp.bfloat16


def kernel_taps():
    offsets = np.arange(2 * HALF + 1).astype(np.float32) - HALF
    gaussian = np.exp(-offsets * offsets / np.float32(18.0))
    centre = np.sum(offsets * offsets * gaussian * gaussian) / np.sum(gaussian * gaussian)
    table = np.stack([gaussian, offsets * gaussian, (offsets * offsets - centre) * gaussian])
    table = table / np.sqrt(np.sum(table * table, axis=1, keepdims=True))
    return table.astype(BF16).astype(np.float32)


def band_matrix(table, lead, trail, displace):
    index = np.arange(trail)[None, :] - np.arange(lead)[:, None] + displace
    inside = (index >= 0) & (index <= 2 * HALF)
    return np.where(inside[None], table[:, np.clip(index, 0, 2 * HALF)], 0.0)


def iota(shape, dim):
    return lax.broadcasted_iota(jnp.int32, shape, dim)


def nn(a, b):
    return jnp.dot(a, b, preferred_element_type=F32)


def nt(a, b):
    return lax.dot_general(a, b, (((1,), (1,)), ((), ())), preferred_element_type=F32)


def tn(a, b):
    return lax.dot_general(a, b, (((0,), (0,)), ((), ())), preferred_element_type=F32)


def each(count, step):
    if count <= 4:
        for k in range(count):
            step(k)
    else:
        def body(k, carry):
            step(k)
            return carry

        lax.fori_loop(0, count, body, 0)


def thirds(value):
    high = value.astype(BF16)
    rest = value - high.astype(F32)
    middle = rest.astype(BF16)
    low = (rest - middle.astype(F32)).astype(BF16)
    return jnp.concatenate([high, middle, low], axis=0)


def kernel(
    visits, strips, bands, distinct,
    images, masks, weight_in, cross_in, owner_in, table_in,
    coadd_out, image_s, basis, mixers, order_out,
    mask_v, image_v, tables, weight, cross, owner, use, use_image, turned, turned_image, send, recv,
    patches, chosen, template_v, owned, prods, small, small_in, lined,
    first_sem, in_sem, const_sem, sum_send, sum_recv, template_send, template_recv, owned_recv,
    st_send, st_recv,
):
    pieces, rows, cols = images.shape[1:]
    blocks = rows // TILE
    chunks = in_sem.shape[1]
    chunk = rows // chunks
    span = pieces * TILE
    cap = pieces // distinct
    halves = cols // LANES
    lead = (visits - halves) // 2
    last = bands - 1
    sheet = distinct * 2 * chunk
    parcel = sheet + TILE
    me = lax.axis_index("visit")
    strip = lax.axis_index("strip")
    band = lax.axis_index("band")
    above = strip > 0
    below = strip < strips - 1
    mine = me - lead
    central = (me >= lead) & (me < lead + halves)
    owning = central & (band == last)
    reach = 1 + above.astype(jnp.int32) + below.astype(jnp.int32)

    firsts = [
        pltpu.make_async_copy(cross_in, cross, first_sem.at[0]),
        pltpu.make_async_copy(owner_in, owner, first_sem.at[1]),
        pltpu.make_async_copy(weight_in, weight, first_sem.at[2]),
    ]
    for copy in firsts:
        copy.start()

    loads = []
    for k in range(chunks):
        part = pl.ds(k * chunk, chunk)
        loads.append((
            pltpu.make_async_copy(masks.at[0, :, part, :], mask_v.at[:, part, :], in_sem.at[0, k]),
            pltpu.make_async_copy(images.at[0, :, part, :], image_v.at[:, part, :], in_sem.at[1, k]),
        ))
        for copy in loads[k]:
            copy.start()

    barrier = pltpu.get_barrier_semaphore()

    def greet(v, hop, b):
        target = {"visit": v, "strip": lax.rem(strip + hop, strips), "band": b}
        pl.semaphore_signal(barrier, inc=1, device_id=target, device_id_type=MESH)

    def near(hop, step):
        if hop == 0:
            step()
        elif hop == 1 and strips == 2:
            step()
        elif hop == 1:
            pl.when(below)(step)
        elif hop == strips - 1:
            pl.when(above)(step)

    def adjoining(hop):
        if hop in (0, 1) and strips == 2:
            return jnp.bool_(True)
        return below if hop == 1 else (above if hop == strips - 1 else jnp.bool_(False))

    @pl.when(owning)
    def _():
        for hop in sorted({0, 1 % strips, strips - 1}):
            def greet_strip():
                def greet_visit(v):
                    for b in range(bands):
                        if hop == 0 and b == last:
                            pl.when(me != v)(functools.partial(greet, v, hop, b))
                        else:
                            greet(v, hop, b)

                each(visits, greet_visit)

            near(hop, greet_strip)
        for hop in range(2, strips - 1):
            greet(me, hop, band)
        for hop in sorted({1 % strips, strips - 1} - {0}):
            if strips > 2:
                pl.when(jnp.logical_not(adjoining(hop)))(functools.partial(greet, me, hop, band))

    @pl.when(jnp.logical_not(owning))
    def _():
        for hop in sorted({0, 1 % strips, strips - 1}):
            def greet_owners():
                for h in range(halves):
                    greet(lead + h, hop, last)

            near(hop, greet_owners)
        for hop in range(1, strips):
            greet(me, hop, band)

    constants = pltpu.make_async_copy(table_in, tables, const_sem)
    constants.start()

    for copy in firsts:
        copy.wait()
    seats = [owner[cross[0, j]] for j in range(pieces)]
    slots = [jnp.int32(0)] * distinct
    rank = jnp.int32(0)
    for q in range(visits):
        present = jnp.int32(0)
        for j in range(pieces):
            present = present | jnp.where(seats[j] == q, 1, 0)
        for d in range(distinct):
            slots[d] = slots[d] + jnp.where((present == 1) & (rank == d), q, 0)
        rank = rank + present

    position = jnp.zeros((1, pieces), jnp.int32)
    for j in range(pieces):
        position = position + jnp.where(iota((1, pieces), 1) == j, seats[j], 0)
    e2 = iota((pieces, span), 0) == jnp.right_shift(iota((pieces, span), 1), 4)
    e2 = e2.astype(F32).astype(BF16)
    pair = jnp.where(
        iota((8, pieces), 0) == 0, weight[...].astype(F32), position.astype(F32)
    ).astype(BF16)
    wide = nn(pair, e2)
    same = (iota((TILE, span), 0) & (TILE - 1)) == (iota((TILE, span), 1) & (TILE - 1))
    adder = jnp.concatenate([
        jnp.where(same & (wide[1:2] == lax.convert_element_type(slots[d], F32)), wide[0:1], 0.0)
        for d in range(distinct)
    ], axis=0).astype(BF16)
    names = jnp.zeros((TILE, LANES), jnp.int32)
    for d in range(distinct):
        names = names + jnp.where(iota((TILE, LANES), 0) == d, slots[d], 0)
    for h in range(halves):
        send[h, 0, pl.ds(sheet, TILE), :] = names.astype(F32).astype(BF16)

    def parcel_at(b, c, v):
        return pl.multiple_of(((b * chunks + c) * visits + v) * parcel, TILE)

    def size(c):
        return parcel if c == 0 else sheet

    def some(count):
        return recv.at[pl.ds(0, count), :]

    def sum_copy(h, b, c):
        return pltpu.make_async_remote_copy(
            src_ref=send.at[h, c, pl.ds(0, size(c)), :],
            dst_ref=recv.at[pl.ds(parcel_at(b, c, me), size(c)), :],
            send_sem=sum_send, recv_sem=sum_recv.at[b, c],
            device_id={"visit": lead + h, "band": last}, device_id_type=MESH,
        )

    def template_copy(b, h, v, d, c):
        return pltpu.make_async_remote_copy(
            src_ref=chosen.at[b, v, d, pl.ds(c * chunk, chunk), :],
            dst_ref=template_v.at[d, h, pl.ds(TILE + c * chunk, chunk), :],
            send_sem=template_send, recv_sem=template_recv.at[d],
            device_id={"visit": v, "band": b}, device_id_type=MESH,
        )

    def edge_copy(way, b, h, v, d):
        step, source, target = ((1, rows - TILE, 0), (strips - 1, 0, rows + TILE))[way]
        return pltpu.make_async_remote_copy(
            src_ref=chosen.at[b, v, d, pl.ds(source, TILE), :],
            dst_ref=template_v.at[d, h, pl.ds(target, TILE), :],
            send_sem=template_send, recv_sem=template_recv.at[d],
            device_id={"visit": v, "strip": lax.rem(strip + step, strips), "band": b},
            device_id_type=MESH,
        )

    def owned_copy(b, h, v):
        return pltpu.make_async_remote_copy(
            src_ref=patches.at[b, v], dst_ref=owned.at[h],
            send_sem=template_send, recv_sem=owned_recv,
            device_id={"visit": v, "band": b}, device_id_type=MESH,
        )

    def wait_for(sem, count):
        pltpu.make_async_copy(some(count), some(count), sem).wait()

    def partial(c):
        for copy in loads[c]:
            copy.wait()
        for t in range(c * chunk // TILE, (c + 1) * chunk // TILE):
            piece_rows = pl.ds(t * TILE, TILE)
            lanes = pl.ds(t * cols, cols)
            usable = (mask_v[:, piece_rows, :].reshape(span, cols) & 3) != 3
            usable = usable.astype(F32).astype(BF16)
            masked = usable * image_v[:, piece_rows, :].reshape(span, cols)
            use[:, :, lanes] = usable.reshape(pieces, TILE, cols)
            use_image[:, :, lanes] = masked.reshape(pieces, TILE, cols)
            for part, value in enumerate((masked, usable)):
                total = nn(adder, value).astype(BF16)
                for d in range(distinct):
                    for h in range(halves):
                        at = (d * 2 + part) * chunk + t * TILE - c * chunk
                        send[h, c, pl.ds(at, TILE), :] = total[
                            d * TILE : (d + 1) * TILE, h * LANES : (h + 1) * LANES
                        ]

    met = jnp.where(
        owning, visits * bands * reach - 1 + strips - reach, halves * reach + strips - 1
    )
    for c in range(chunks):
        partial(c)
        if c == 0:
            pl.semaphore_wait(barrier, met)
        for b in range(bands):
            for h in range(halves):
                @pl.when((band == b) & jnp.logical_not(owning & (mine == h)))
                def _():
                    sum_copy(h, b, c).start()

    @pl.when(jnp.logical_not(above))
    def _():
        template_v[:, :, pl.ds(0, TILE), :] = jnp.zeros((distinct, halves, TILE, LANES), BF16)

    @pl.when(jnp.logical_not(below))
    def _():
        template_v[:, :, pl.ds(rows + TILE, TILE), :] = jnp.zeros(
            (distinct, halves, TILE, LANES), BF16
        )

    def reduce(b, c):
        if b == last:
            recv[pl.ds(parcel_at(b, c, me), parcel), :] = send[mine, c]
        wait_for(sum_recv.at[b, c], (visits if b != last else visits - 1) * size(c))

        def id_tile(v, d):
            names = recv[pl.ds(parcel_at(b, 0, v) + sheet, TILE), :].astype(F32)
            return jnp.broadcast_to(names[d : d + 1], (TILE, LANES))

        def value(v, d, part, t):
            at = (d * 2 + part) * chunk + t * TILE - c * chunk
            start = pl.multiple_of(parcel_at(b, c, v) + at, TILE)
            return recv[pl.ds(start, TILE), :].astype(F32)

        def one_tile(t):
            piece_rows = pl.ds(t * TILE, TILE)
            if visits <= 4:
                tiles = [[id_tile(v, d) for d in range(distinct)] for v in range(visits)]
                finals = []
                for q in range(visits):
                    numerator = jnp.zeros((TILE, LANES), F32)
                    denominator = jnp.zeros((TILE, LANES), F32)
                    for v in range(visits):
                        for d in range(distinct):
                            here = tiles[v][d] == float(q)
                            numerator += jnp.where(here, value(v, d, 0, t), 0.0)
                            denominator += jnp.where(here, value(v, d, 1, t), 0.0)
                    final = numerator / jnp.maximum(denominator, 1.0)
                    patches[b, q, piece_rows, :] = final.astype(BF16)
                    finals.append(final)
                for v in range(visits):
                    for d in range(distinct):
                        picked = finals[0]
                        for q in range(1, visits):
                            picked = jnp.where(tiles[v][d] == float(q), finals[q], picked)
                        chosen[b, v, d, piece_rows, :] = picked.astype(BF16)
                return

            def one_patch(q):
                number = lax.convert_element_type(q, F32)

                def add(v, carry):
                    numerator, denominator = carry
                    for d in range(distinct):
                        here = id_tile(v, d) == number
                        numerator += jnp.where(here, value(v, d, 0, t), 0.0)
                        denominator += jnp.where(here, value(v, d, 1, t), 0.0)
                    return numerator, denominator

                zero = jnp.zeros((TILE, LANES), F32)
                numerator, denominator = lax.fori_loop(0, visits, add, (zero, zero))
                final = numerator / jnp.maximum(denominator, 1.0)
                patches[b, q, piece_rows, :] = final.astype(BF16)

            def pick(v):
                for d in range(distinct):
                    tile = id_tile(v, d)

                    def better(q, picked):
                        final = patches[b, q, piece_rows, :].astype(F32)
                        return jnp.where(tile == lax.convert_element_type(q, F32), final, picked)

                    picked = lax.fori_loop(0, visits, better, jnp.zeros((TILE, LANES), F32))
                    chosen[b, v, d, piece_rows, :] = picked.astype(BF16)

            each(visits, one_patch)
            each(visits, pick)

        for t in range(c * chunk // TILE, (c + 1) * chunk // TILE):
            one_tile(t)

        for d in range(distinct):
            def templates(v):
                if c == chunks - 1:
                    pl.when(below)(edge_copy(0, b, mine, v, d).start)
                if c == 0:
                    pl.when(above)(edge_copy(1, b, mine, v, d).start)
                if b == last:
                    pl.when(me != v)(template_copy(b, mine, v, d, c).start)
                else:
                    template_copy(b, mine, v, d, c).start()

            each(visits, templates)

    @pl.when(owning)
    def _():
        for c in range(chunks):
            for b in range(bands):
                reduce(b, c)
        template_v[:, mine, pl.ds(TILE, rows), :] = chosen[last, me]

        def owners(v):
            for b in range(bands):
                if b == last:
                    pl.when(me != v)(owned_copy(b, mine, v).start)
                else:
                    owned_copy(b, mine, v).start()

        each(visits, owners)
        owned[mine] = patches[last, me]

    places = []
    for d in range(distinct):
        count = jnp.int32(0)
        found = [jnp.int32(0)] * cap
        for j in range(pieces):
            hit = seats[j] == slots[d]
            for k in range(cap):
                found[k] = found[k] + jnp.where(hit & (count == k), j, 0)
            count = count + jnp.where(hit, 1, 0)
        places += found
    order = jnp.zeros((1, LANES), jnp.int32)
    for k in range(pieces):
        order = order + jnp.where(iota((1, LANES), 1) == k, places[k], 0)
        for t in range(blocks):
            image_s[t, k] = image_v[places[k], pl.ds(t * TILE, TILE), :]
    order_out[...] = order
    for d in range(distinct):
        for t in range(blocks):
            lanes = pl.ds(t * cols, cols)
            for source, target in ((use, turned), (use_image, turned_image)):
                stack = [source[places[d * cap + k], :, lanes] for k in range(cap)]
                target[d, lanes, :] = jnp.transpose(jnp.concatenate(stack, axis=0))
    constants.wait()

    up_top = BASES // 2 * cols
    vertical = tables[pl.ds(up_top, 3 * rows), pl.ds(0, rows + 2 * TILE)]

    def across(c):
        return tables[pl.ds(c * cols, cols), pl.ds(0, cols)]

    wide_n = len(pairs) * TILE
    wide_b = BASES * TILE
    lines = lined.shape[0]

    def kept(values):
        keep = (iota(values.shape, 0) & (TILE - 1)) == (iota(values.shape, 1) & (TILE - 1))
        return jnp.where(keep, values, 0.0)

    system = jnp.zeros((lines, LANES), F32)
    for d in range(distinct):
        for local in (False, True):
            for sides in range(3 if strips > 2 else 2):
                count = (halves - local) * rows + halves * sides * TILE

                @pl.when((owning == local) & (reach == sides + 1))
                def _():
                    if count:
                        wait_for(template_recv.at[d], count)

        template = jnp.concatenate([template_v[d, h] for h in range(halves)], axis=1)
        smooth = nn(vertical, template).astype(BF16)
        planes = [None] * BASES
        for c in range(3):
            taken = [a for a in range(BASES) if basis_cols[a] == c]
            product = nn(smooth[: len(taken) * rows], across(c)).astype(BF16)
            for a in taken:
                r = basis_rows[a]
                planes[a] = product[r * rows : (r + 1) * rows]
        for a in range(BASES):
            for t in range(blocks):
                basis[d, pl.ds(a * TILE, TILE), pl.ds(t * cols, cols)] = planes[a][
                    t * TILE : (t + 1) * TILE
                ]
        for n, (a, c) in enumerate(pairs):
            product = planes[a] * planes[c]
            for t in range(blocks):
                prods[pl.ds(n * TILE, TILE), pl.ds(t * cols, cols)] = product[
                    t * TILE : (t + 1) * TILE
                ]
        sums = jnp.concatenate([
            kept(nn(prods[...], turned[d])),
            kept(nn(basis[d], turned_image[d])),
            jnp.zeros((lines * TILE - wide_n - wide_b, cap * TILE), F32),
        ], axis=0)
        sums = jnp.sum(sums.reshape(lines, TILE, cap * TILE), axis=1)
        collect = jnp.right_shift(iota((cap * TILE, LANES), 0), 4) + d * cap
        collect = (collect == iota((cap * TILE, LANES), 1)).astype(F32).astype(BF16)
        gathered = nn(thirds(sums), collect)
        system = system + sum(gathered[k * lines : (k + 1) * lines] for k in range(3))
    groups = lines // 8
    small[...] = sum(
        pltpu.roll(system[g * 8 : (g + 1) * 8], g * pieces, 1) if g else system[:8]
        for g in range(groups)
    )
    exchanges = []
    for hop in range(1, strips):
        exchanges.append(pltpu.make_async_remote_copy(
            src_ref=small, dst_ref=small_in.at[hop - 1],
            send_sem=st_send, recv_sem=st_recv,
            device_id={"strip": lax.rem(strip + hop, strips)}, device_id_type=MESH,
        ))
    for copy in exchanges:
        copy.start()

    wide_c = 2 * wide_b
    column = iota((16, wide_c), 1)
    source = jnp.where(
        column < wide_b, jnp.right_shift(column, 4), jnp.right_shift(column - wide_b, 4) + 8
    )
    e3 = (source == iota((16, wide_c), 0)).astype(F32).astype(BF16)
    diagonal = iota((TILE, wide_c), 0) == (iota((TILE, wide_c), 1) & (TILE - 1))

    for local in (False, True):
        @pl.when(owning == local)
        def _():
            if halves - local:
                wait_for(owned_recv, (halves - local) * rows)
    for h in range(halves):
        coadd_out[:, pl.ds(h * LANES, LANES)] = owned[h]

    if exchanges:
        pltpu.make_async_copy(small_in, small_in, st_recv).wait()

    full = small[...]
    for hop in range(1, strips):
        full = full + small_in[hop - 1]
    for g in range(groups):
        lined[pl.ds(g * 8, 8), :] = pltpu.roll(full, LANES - g * pieces, 1) if g else full

    def line_of(n):
        return lined[pl.ds(n, 1), :]

    entry = {pairs[n]: line_of(n) + float(pairs[n][0] == pairs[n][1]) for n in range(len(pairs))}
    side = [line_of(len(pairs) + a) for a in range(BASES)]
    inverse = [None] * BASES
    for k in range(BASES):
        inverse[k] = 1.0 / entry[k, k]
        for i in range(k + 1, BASES):
            factor = entry[k, i] * inverse[k]
            for c in range(i, BASES):
                entry[i, c] = entry[i, c] - factor * entry[k, c]
            side[i] = side[i] - factor * side[k]
    for k in reversed(range(BASES)):
        for c in range(k + 1, BASES):
            side[k] = side[k] - entry[k, c] * side[c]
        side[k] = side[k] * inverse[k]
    found = jnp.zeros((8, LANES), F32)
    for a in range(BASES):
        found = found + jnp.where(iota((8, LANES), 0) == a, side[a], 0.0)
    high = found.astype(BF16).astype(F32)
    low = found - high
    both = jnp.concatenate([high, low], axis=0)[:, :pieces].astype(BF16)
    spread = tn(both, e3)
    for k in range(pieces):
        mixers[k // cap, pl.ds(k % cap * TILE, TILE), :] = jnp.where(
            diagonal, spread[k : k + 1], 0.0
        ).astype(BF16)

    for copy in exchanges:
        copy.wait_send()
    for local in (False, True):
        @pl.when(owning == local)
        def _():
            if halves - local:
                wait_for(sum_send, (halves - local) * sum(size(c) for c in range(chunks)))
    for sides in range(3 if strips > 2 else 2):
        mains = (bands * visits - 1) * (distinct + 1) * rows
        edges = bands * visits * distinct * sides * TILE

        @pl.when(owning & (reach == sides + 1))
        def _():
            wait_for(template_send, mains + edges)


def finish(coadd_in, image_s, basis, mixers, order, coadd_out, diff_out, diff_v, out_sem):
    distinct = basis.shape[0]
    blocks, pieces, _, cols = image_s.shape
    cap = pieces // distinct
    stores = [pltpu.make_async_copy(coadd_in, coadd_out.at[0, 0], out_sem.at[0])]
    stores[0].start()
    places = [order[0, k] for k in range(pieces)]
    for t in range(blocks):
        lanes = pl.ds(t * cols, cols)
        for d in range(distinct):
            planes = basis[d, :, lanes]
            fitted = nn(mixers[d], jnp.concatenate([planes, planes], axis=0))
            for k in range(cap):
                value = image_s[t, d * cap + k].astype(F32) - fitted[k * TILE : (k + 1) * TILE]
                diff_v[t, places[d * cap + k]] = value.astype(BF16)
        copy = pltpu.make_async_copy(
            diff_v.at[t], diff_out.at[0, :, pl.ds(t * TILE, TILE), :], out_sem.at[1 + t]
        )
        copy.start()
        stores.append(copy)
    for copy in stores:
        copy.wait()


def body(visits, strips, bands, images, mask_bits, visit_weight, intersection, patch_owner):
    _, pieces, rows, cols = images.shape
    blocks = rows // TILE
    halves = cols // LANES
    distinct = max(1, patch_owner.shape[0] // 2)
    cap = pieces // distinct
    taps = kernel_taps()
    width = -(-max(LANES, cols, rows + 2 * TILE) // LANES) * LANES
    tables = jnp.asarray(np.concatenate([
        np.pad(part, ((0, 0), (0, width - part.shape[1])))
        for part in (
            np.transpose(band_matrix(taps, cols, cols, HALF), (0, 2, 1)).reshape(3 * cols, cols),
            band_matrix(taps, rows, rows + 2 * TILE, HALF - TILE).reshape(3 * rows, -1),
        )
    ]), BF16)
    hbm = pl.BlockSpec(memory_space=pltpu.HBM)
    vmem = pl.BlockSpec(memory_space=pltpu.VMEM)
    dma = pltpu.SemaphoreType.DMA
    cross = intersection.reshape(1, pieces)
    others = max(1, strips - 1)
    chunks = 2
    parcel = distinct * 2 * rows // chunks + TILE
    lines = -(-(len(pairs) + BASES) // 8) * 8
    middle = pl.pallas_call(
        functools.partial(kernel, visits, strips, bands, distinct),
        out_shape=(
            jax.ShapeDtypeStruct((rows, cols), BF16),
            jax.ShapeDtypeStruct((blocks, pieces, TILE, cols), BF16),
            jax.ShapeDtypeStruct((distinct, BASES * TILE, blocks * cols), BF16),
            jax.ShapeDtypeStruct((distinct, cap * TILE, 2 * BASES * TILE), BF16),
            jax.ShapeDtypeStruct((1, LANES), jnp.int32),
        ),
        in_specs=[hbm, hbm, hbm, hbm, hbm, hbm],
        out_specs=(vmem, vmem, vmem, vmem, vmem),
        scratch_shapes=[
            pltpu.VMEM((pieces, rows, cols), jnp.int32),
            pltpu.VMEM((pieces, rows, cols), BF16),
            pltpu.VMEM(tables.shape, BF16),
            pltpu.VMEM((1, pieces), BF16),
            pltpu.SMEM((1, pieces), jnp.int32),
            pltpu.SMEM(patch_owner.shape, jnp.int32),
            pltpu.VMEM((pieces, TILE, blocks * cols), BF16),
            pltpu.VMEM((pieces, TILE, blocks * cols), BF16),
            pltpu.VMEM((distinct, blocks * cols, cap * TILE), BF16),
            pltpu.VMEM((distinct, blocks * cols, cap * TILE), BF16),
            pltpu.VMEM((halves, chunks, parcel, LANES), BF16),
            pltpu.VMEM((bands * chunks * visits * parcel, LANES), BF16),
            pltpu.VMEM((bands, visits, rows, LANES), BF16),
            pltpu.VMEM((bands, visits, distinct, rows, LANES), BF16),
            pltpu.VMEM((distinct, halves, rows + 2 * TILE, LANES), BF16),
            pltpu.VMEM((halves, rows, LANES), BF16),
            pltpu.VMEM((len(pairs) * TILE, blocks * cols), BF16),
            pltpu.VMEM((8, LANES), F32),
            pltpu.VMEM((others, 8, LANES), F32),
            pltpu.VMEM((lines, LANES), F32),
            dma((3,)),
            dma((2, chunks)),
            dma,
            dma,
            dma((bands, chunks)),
            dma,
            dma((distinct,)),
            dma,
            dma,
            dma,
        ],
        compiler_params=pltpu.CompilerParams(
            collective_id=0, has_side_effects=True, vmem_limit_bytes=40_000_000
        ),
        name="coadd_solve",
    )(*(
        pltpu.with_memory_space_constraint(part, pltpu.HBM)
        for part in (images, mask_bits, visit_weight, cross, patch_owner, tables)
    ))
    return pl.pallas_call(
        finish,
        out_shape=(
            jax.ShapeDtypeStruct((1, 1, rows, cols), BF16),
            jax.ShapeDtypeStruct(images.shape, BF16),
        ),
        in_specs=[vmem, vmem, vmem, vmem, vmem],
        out_specs=(hbm, hbm),
        scratch_shapes=[
            pltpu.VMEM((blocks, pieces, TILE, cols), BF16),
            dma((1 + blocks,)),
        ],
        compiler_params=pltpu.CompilerParams(vmem_limit_bytes=40 * 1024 * 1024),
        name="difference",
    )(*middle)


def solution(mesh):
    in_specs = (
        P("band", ("groups", "visit"), "strip", None),
        P("band", ("groups", "visit"), "strip", None),
        P("band", ("groups", "visit")),
        P(("groups", "visit"), None),
        P("groups"),
    )
    out_specs = (
        P("band", ("groups", "visit"), "strip", None),
        P("band", ("groups", "visit"), "strip", None),
    )
    step = functools.partial(
        body, mesh.shape["visit"], mesh.shape["strip"], mesh.shape["band"]
    )
    return jax.shard_map(step, mesh=mesh, in_specs=in_specs, out_specs=out_specs, check_vma=False)
```

```python
import functools

import jax
import jax.numpy as jnp
import numpy as np
from jax import lax
from jax.experimental import pallas as pl
from jax.experimental.pallas import tpu as pltpu
from jax.sharding import PartitionSpec as P

BASES = 6
HALF = 9
TILE = 16
LANES = 128

basis_rows = (0, 0, 1, 0, 2, 1)
basis_cols = (0, 1, 0, 2, 0, 1)
pairs = tuple((a, c) for a in range(BASES) for c in range(a, BASES))
MESH = pl.DeviceIdType.MESH
F32 = jnp.float32
BF16 = jnp.bfloat16


def kernel_taps():
    offsets = np.arange(2 * HALF + 1).astype(np.float32) - HALF
    gaussian = np.exp(-offsets * offsets / np.float32(18.0))
    centre = np.sum(offsets * offsets * gaussian * gaussian) / np.sum(gaussian * gaussian)
    table = np.stack([gaussian, offsets * gaussian, (offsets * offsets - centre) * gaussian])
    table = table / np.sqrt(np.sum(table * table, axis=1, keepdims=True))
    return table.astype(BF16).astype(np.float32)


def band_matrix(table, lead, trail, displace):
    index = np.arange(trail)[None, :] - np.arange(lead)[:, None] + displace
    inside = (index >= 0) & (index <= 2 * HALF)
    return np.where(inside[None], table[:, np.clip(index, 0, 2 * HALF)], 0.0)


def iota(shape, dim):
    return lax.broadcasted_iota(jnp.int32, shape, dim)


def nn(a, b):
    return jnp.dot(a, b, preferred_element_type=F32)


def nt(a, b):
    return lax.dot_general(a, b, (((1,), (1,)), ((), ())), preferred_element_type=F32)


def tn(a, b):
    return lax.dot_general(a, b, (((0,), (0,)), ((), ())), preferred_element_type=F32)


def each(count, step):
    if count <= 4:
        for k in range(count):
            step(k)
    else:
        def body(k, carry):
            step(k)
            return carry

        lax.fori_loop(0, count, body, 0)


def thirds(value):
    high = value.astype(BF16)
    rest = value - high.astype(F32)
    middle = rest.astype(BF16)
    low = (rest - middle.astype(F32)).astype(BF16)
    return jnp.concatenate([high, middle, low], axis=0)


def kernel(
    visits, strips, bands, distinct,
    images, masks, weight_in, cross_in, owner_in, table_in,
    coadd_out, image_s, basis, mixers, order_out,
    mask_v, image_v, tables, weight, cross, owner, use, use_image, turned, turned_image, send, recv,
    patches, chosen, template_v, owned, prods, small, small_in, lined,
    first_sem, in_sem, const_sem, sum_send, sum_recv, template_send, template_recv, owned_recv,
    st_send, st_recv,
):
    pieces, rows, cols = images.shape[1:]
    blocks = rows // TILE
    chunks = sum_recv.shape[1]
    parts = in_sem.shape[1]
    chunk = rows // chunks
    span = pieces * TILE
    cap = pieces // distinct
    halves = cols // LANES
    lead = (visits - halves) // 2
    last = bands - 1
    sheet = distinct * 2 * chunk
    parcel = sheet + TILE
    me = lax.axis_index("visit")
    strip = lax.axis_index("strip")
    band = lax.axis_index("band")
    above = strip > 0
    below = strip < strips - 1
    mine = me - lead
    late = me * 2 >= visits
    central = (me >= lead) & (me < lead + halves)
    owning = central & (band == last)
    reach = 1 + above.astype(jnp.int32) + below.astype(jnp.int32)

    firsts = [
        pltpu.make_async_copy(cross_in, cross, first_sem.at[0]),
        pltpu.make_async_copy(owner_in, owner, first_sem.at[1]),
        pltpu.make_async_copy(weight_in, weight, first_sem.at[2]),
    ]
    for copy in firsts:
        copy.start()

    loads = []
    for k in range(parts):
        part = pl.ds(k * rows // parts, rows // parts)
        loads.append((
            pltpu.make_async_copy(masks.at[0, :, part, :], mask_v.at[:, part, :], in_sem.at[0, k]),
            pltpu.make_async_copy(images.at[0, :, part, :], image_v.at[:, part, :], in_sem.at[1, k]),
        ))
        for copy in loads[k]:
            copy.start()

    barrier = pltpu.get_barrier_semaphore()

    def greet(v, hop, b):
        target = {"visit": v, "strip": lax.rem(strip + hop, strips), "band": b}
        pl.semaphore_signal(barrier, inc=1, device_id=target, device_id_type=MESH)

    def near(hop, step):
        if hop == 0:
            step()
        elif hop == 1 and strips == 2:
            step()
        elif hop == 1:
            pl.when(below)(step)
        elif hop == strips - 1:
            pl.when(above)(step)

    def adjoining(hop):
        if hop in (0, 1) and strips == 2:
            return jnp.bool_(True)
        return below if hop == 1 else (above if hop == strips - 1 else jnp.bool_(False))

    @pl.when(owning)
    def _():
        for hop in sorted({0, 1 % strips, strips - 1}):
            def greet_strip():
                def greet_visit(v):
                    for b in range(bands):
                        if hop == 0 and b == last:
                            pl.when(me != v)(functools.partial(greet, v, hop, b))
                        else:
                            greet(v, hop, b)

                each(visits, greet_visit)

            near(hop, greet_strip)
        for hop in range(2, strips - 1):
            greet(me, hop, band)
        for hop in sorted({1 % strips, strips - 1} - {0}):
            if strips > 2:
                pl.when(jnp.logical_not(adjoining(hop)))(functools.partial(greet, me, hop, band))

    @pl.when(jnp.logical_not(owning))
    def _():
        for hop in sorted({0, 1 % strips, strips - 1}):
            def greet_owners():
                for h in range(halves):
                    greet(lead + h, hop, last)

            near(hop, greet_owners)
        for hop in range(1, strips):
            greet(me, hop, band)

    constants = pltpu.make_async_copy(table_in, tables, const_sem)
    constants.start()

    for copy in firsts:
        copy.wait()
    seats = [owner[cross[0, j]] for j in range(pieces)]
    slots = [jnp.int32(0)] * distinct
    rank = jnp.int32(0)
    for q in range(visits):
        present = jnp.int32(0)
        for j in range(pieces):
            present = present | jnp.where(seats[j] == q, 1, 0)
        for d in range(distinct):
            slots[d] = slots[d] + jnp.where((present == 1) & (rank == d), q, 0)
        rank = rank + present

    position = jnp.zeros((1, pieces), jnp.int32)
    for j in range(pieces):
        position = position + jnp.where(iota((1, pieces), 1) == j, seats[j], 0)
    e2 = iota((pieces, span), 0) == jnp.right_shift(iota((pieces, span), 1), 4)
    e2 = e2.astype(F32).astype(BF16)
    pair = jnp.where(
        iota((8, pieces), 0) == 0, weight[...].astype(F32), position.astype(F32)
    ).astype(BF16)
    wide = nn(pair, e2)
    same = (iota((TILE, span), 0) & (TILE - 1)) == (iota((TILE, span), 1) & (TILE - 1))
    adder = jnp.concatenate([
        jnp.where(same & (wide[1:2] == lax.convert_element_type(slots[d], F32)), wide[0:1], 0.0)
        for d in range(distinct)
    ], axis=0).astype(BF16)
    names = jnp.zeros((TILE, LANES), jnp.int32)
    for d in range(distinct):
        names = names + jnp.where(iota((TILE, LANES), 0) == d, slots[d], 0)
    for h in range(halves):
        send[h, 0, pl.ds(sheet, TILE), :] = names.astype(F32).astype(BF16)

    def parcel_at(b, c, v):
        return pl.multiple_of(((b * chunks + c) * visits + v) * parcel, TILE)

    def size(c):
        return parcel if c == 0 else sheet

    def some(count):
        return recv.at[pl.ds(0, count), :]

    def sum_copy(h, c):
        return pltpu.make_async_remote_copy(
            src_ref=send.at[h, c, pl.ds(0, size(c)), :],
            dst_ref=recv.at[pl.ds(parcel_at(band, c, me), size(c)), :],
            send_sem=sum_send, recv_sem=sum_recv.at[band, c],
            device_id={"visit": lead + h, "band": last}, device_id_type=MESH,
        )

    def template_copy(b, h, v, c):
        return pltpu.make_async_remote_copy(
            src_ref=chosen.at[b, v, :, pl.ds(c * chunk, chunk), :],
            dst_ref=template_v.at[h, :, pl.ds(TILE + c * chunk, chunk), :],
            send_sem=template_send, recv_sem=template_recv,
            device_id={"visit": v, "band": b}, device_id_type=MESH,
        )

    def edge_copy(way, b, h, v):
        step, source, target = ((1, rows - TILE, 0), (strips - 1, 0, rows + TILE))[way]
        return pltpu.make_async_remote_copy(
            src_ref=chosen.at[b, v, :, pl.ds(source, TILE), :],
            dst_ref=template_v.at[h, :, pl.ds(target, TILE), :],
            send_sem=template_send, recv_sem=template_recv,
            device_id={"visit": v, "strip": lax.rem(strip + step, strips), "band": b},
            device_id_type=MESH,
        )

    def owned_copy(b, h, v):
        return pltpu.make_async_remote_copy(
            src_ref=patches.at[b, v], dst_ref=owned.at[h],
            send_sem=template_send, recv_sem=owned_recv,
            device_id={"visit": v, "band": b}, device_id_type=MESH,
        )

    def wait_for(sem, count):
        pltpu.make_async_copy(some(count), some(count), sem).wait()

    def partial(c):
        if c * parts % chunks == 0:
            for copy in loads[c * parts // chunks]:
                copy.wait()
        for t in range(c * chunk // TILE, (c + 1) * chunk // TILE):
            piece_rows = pl.ds(t * TILE, TILE)
            lanes = pl.ds(t * cols, cols)
            usable = (mask_v[:, piece_rows, :].reshape(span, cols) & 3) != 3
            usable = usable.astype(F32).astype(BF16)
            masked = usable * image_v[:, piece_rows, :].reshape(span, cols)
            use[:, :, lanes] = usable.reshape(pieces, TILE, cols)
            use_image[:, :, lanes] = masked.reshape(pieces, TILE, cols)
            for part, value in enumerate((masked, usable)):
                total = nn(adder, value).astype(BF16)
                for d in range(distinct):
                    for h in range(halves):
                        at = (d * 2 + part) * chunk + t * TILE - c * chunk
                        send[h, c, pl.ds(at, TILE), :] = total[
                            d * TILE : (d + 1) * TILE, h * LANES : (h + 1) * LANES
                        ]

    met = jnp.where(
        owning, visits * bands * reach - 1 + strips - reach, halves * reach + strips - 1
    )
    for c in range(chunks):
        partial(c)
        if c == 0:
            pl.semaphore_wait(barrier, met)
        for k in range(halves):
            h = jnp.where(late, k, halves - 1 - k)
            pl.when(jnp.logical_not(owning & (mine == h)))(sum_copy(h, c).start)

    @pl.when(jnp.logical_not(above))
    def _():
        template_v[:, :, pl.ds(0, TILE), :] = jnp.zeros((halves, distinct, TILE, LANES), BF16)

    @pl.when(jnp.logical_not(below))
    def _():
        template_v[:, :, pl.ds(rows + TILE, TILE), :] = jnp.zeros(
            (halves, distinct, TILE, LANES), BF16
        )

    def visit_all(act, others_only=False):
        if visits > 4:
            each(visits - others_only, lambda k: act(lax.rem(me + others_only + k, visits)))
            return
        hops = sorted(range(visits), key=lambda k: (abs(k - visits // 2), -k))
        for k in hops:
            if k or not others_only:
                act(lax.rem(me + jnp.where(late, visits - k, k), visits))

    def reduce(b, c):
        if b == last:
            recv[pl.ds(parcel_at(b, c, me), parcel), :] = send[mine, c]
        wait_for(sum_recv.at[b, c], (visits if b != last else visits - 1) * size(c))

        def id_tile(v, d):
            names = recv[pl.ds(parcel_at(b, 0, v) + sheet, TILE), :].astype(F32)
            return jnp.broadcast_to(names[d : d + 1], (TILE, LANES))

        def value(v, d, part, t):
            at = (d * 2 + part) * chunk + t * TILE - c * chunk
            start = pl.multiple_of(parcel_at(b, c, v) + at, TILE)
            return recv[pl.ds(start, TILE), :].astype(F32)

        def one_tile(t):
            piece_rows = pl.ds(t * TILE, TILE)
            if visits <= 4:
                tiles = [[id_tile(v, d) for d in range(distinct)] for v in range(visits)]
                finals = []
                for q in range(visits):
                    numerator = jnp.zeros((TILE, LANES), F32)
                    denominator = jnp.zeros((TILE, LANES), F32)
                    for v in range(visits):
                        for d in range(distinct):
                            here = tiles[v][d] == float(q)
                            numerator += jnp.where(here, value(v, d, 0, t), 0.0)
                            denominator += jnp.where(here, value(v, d, 1, t), 0.0)
                    final = numerator / jnp.maximum(denominator, 1.0)
                    patches[b, q, piece_rows, :] = final.astype(BF16)
                    finals.append(final)
                for v in range(visits):
                    for d in range(distinct):
                        picked = finals[0]
                        for q in range(1, visits):
                            picked = jnp.where(tiles[v][d] == float(q), finals[q], picked)
                        chosen[b, v, d, piece_rows, :] = picked.astype(BF16)
                return

            def one_patch(q):
                number = lax.convert_element_type(q, F32)

                def add(v, carry):
                    numerator, denominator = carry
                    for d in range(distinct):
                        here = id_tile(v, d) == number
                        numerator += jnp.where(here, value(v, d, 0, t), 0.0)
                        denominator += jnp.where(here, value(v, d, 1, t), 0.0)
                    return numerator, denominator

                zero = jnp.zeros((TILE, LANES), F32)
                numerator, denominator = lax.fori_loop(0, visits, add, (zero, zero))
                final = numerator / jnp.maximum(denominator, 1.0)
                patches[b, q, piece_rows, :] = final.astype(BF16)

            def pick(v):
                for d in range(distinct):
                    tile = id_tile(v, d)

                    def better(q, picked):
                        final = patches[b, q, piece_rows, :].astype(F32)
                        return jnp.where(tile == lax.convert_element_type(q, F32), final, picked)

                    picked = lax.fori_loop(0, visits, better, jnp.zeros((TILE, LANES), F32))
                    chosen[b, v, d, piece_rows, :] = picked.astype(BF16)

            each(visits, one_patch)
            each(visits, pick)

        for t in range(c * chunk // TILE, (c + 1) * chunk // TILE):
            one_tile(t)

        if c == chunks - 1:
            @pl.when(below)
            def _():
                visit_all(lambda v: edge_copy(0, b, mine, v).start())

        if c == 0:
            @pl.when(above)
            def _():
                visit_all(lambda v: edge_copy(1, b, mine, v).start())

        visit_all(lambda v: template_copy(b, mine, v, c).start(), b == last)

    @pl.when(owning)
    def _():
        for c in range(chunks):
            for b in range(bands):
                reduce(b, c)
        template_v[mine, :, pl.ds(TILE, rows), :] = chosen[last, me]
        for b in range(bands):
            visit_all(lambda v: owned_copy(b, mine, v).start(), b == last)
        owned[mine] = patches[last, me]

    places = []
    for d in range(distinct):
        count = jnp.int32(0)
        found = [jnp.int32(0)] * cap
        for j in range(pieces):
            hit = seats[j] == slots[d]
            for k in range(cap):
                found[k] = found[k] + jnp.where(hit & (count == k), j, 0)
            count = count + jnp.where(hit, 1, 0)
        places += found
    order = jnp.zeros((1, LANES), jnp.int32)
    for k in range(pieces):
        order = order + jnp.where(iota((1, LANES), 1) == k, places[k], 0)
        for t in range(blocks):
            image_s[t, k] = image_v[places[k], pl.ds(t * TILE, TILE), :]
    order_out[...] = order
    for d in range(distinct):
        for t in range(blocks):
            lanes = pl.ds(t * cols, cols)
            for source, target in ((use, turned), (use_image, turned_image)):
                stack = [source[places[d * cap + k], :, lanes] for k in range(cap)]
                target[d, lanes, :] = jnp.transpose(jnp.concatenate(stack, axis=0))
    constants.wait()

    up_top = BASES // 2 * cols
    vertical = tables[pl.ds(up_top, 3 * rows), pl.ds(0, rows + 2 * TILE)]

    def across(c):
        return tables[pl.ds(c * cols, cols), pl.ds(0, cols)]

    wide_n = len(pairs) * TILE
    wide_b = BASES * TILE
    lines = lined.shape[0]

    for local in (False, True):
        for sides in range(3 if strips > 2 else 2):
            count = distinct * ((halves - local) * rows + halves * sides * TILE)

            @pl.when((owning == local) & (reach == sides + 1))
            def _():
                if count:
                    wait_for(template_recv, count)

    corner = iota((1, TILE, cap * TILE), 1) == (iota((1, TILE, cap * TILE), 2) & (TILE - 1))
    smooth = nn(vertical, jnp.concatenate(
        [template_v[h, d] for d in range(distinct) for h in range(halves)], axis=1
    )).astype(BF16)
    planes = [[None] * BASES for _ in range(distinct)]
    for c in range(3):
        taken = [a for a in range(BASES) if basis_cols[a] == c]
        height = len(taken) * rows
        product = nn(jnp.concatenate(
            [smooth[:height, d * cols : (d + 1) * cols] for d in range(distinct)], axis=0
        ), across(c)).astype(BF16)
        for d in range(distinct):
            for a in taken:
                top = d * height + basis_rows[a] * rows
                planes[d][a] = product[top : top + rows]
    for d in range(distinct):
        for a in range(BASES):
            for t in range(blocks):
                basis[d, pl.ds(a * TILE, TILE), pl.ds(t * cols, cols)] = planes[d][a][
                    t * TILE : (t + 1) * TILE
                ]
        for n, (a, c) in enumerate(pairs):
            product = planes[d][a] * planes[d][c]
            for t in range(blocks):
                prods[d, pl.ds(n * TILE, TILE), pl.ds(t * cols, cols)] = product[
                    t * TILE : (t + 1) * TILE
                ]

    groups = lines // 8
    folded = []
    for d in range(distinct):
        sums = jnp.concatenate([
            nn(prods[d], turned[d]),
            nn(basis[d], turned_image[d]),
            jnp.zeros((lines * TILE - wide_n - wide_b, cap * TILE), F32),
        ], axis=0).reshape(lines, TILE, cap * TILE)
        folded.append(jnp.sum(jnp.where(corner, sums, 0.0), axis=1))
    collect = jnp.concatenate([
        jnp.right_shift(iota((cap * TILE, LANES), 0), 4) + d * cap for d in range(distinct)
    ], axis=0)
    collect = (collect == iota(collect.shape, 1)).astype(F32).astype(BF16)
    gathered = nn(thirds(jnp.concatenate(folded, axis=1)), collect)
    system = sum(gathered[k * lines : (k + 1) * lines] for k in range(3))
    small[...] = sum(
        pltpu.roll(system[g * 8 : (g + 1) * 8], g * pieces, 1) if g else system[:8]
        for g in range(groups)
    )
    exchanges = []
    for hop in range(1, strips):
        exchanges.append(pltpu.make_async_remote_copy(
            src_ref=small, dst_ref=small_in.at[hop - 1],
            send_sem=st_send, recv_sem=st_recv,
            device_id={"strip": lax.rem(strip + hop, strips)}, device_id_type=MESH,
        ))
    for copy in exchanges:
        copy.start()

    wide_c = 2 * wide_b
    column = iota((16, wide_c), 1)
    source = jnp.where(
        column < wide_b, jnp.right_shift(column, 4), jnp.right_shift(column - wide_b, 4) + 8
    )
    e3 = (source == iota((16, wide_c), 0)).astype(F32).astype(BF16)
    diagonal = iota((TILE, wide_c), 0) == (iota((TILE, wide_c), 1) & (TILE - 1))

    for local in (False, True):
        @pl.when(owning == local)
        def _():
            if halves - local:
                wait_for(owned_recv, (halves - local) * rows)
    for h in range(halves):
        coadd_out[:, pl.ds(h * LANES, LANES)] = owned[h]

    if exchanges:
        pltpu.make_async_copy(small_in, small_in, st_recv).wait()

    full = small[...]
    for hop in range(1, strips):
        full = full + small_in[hop - 1]
    for g in range(groups):
        lined[pl.ds(g * 8, 8), :] = pltpu.roll(full, LANES - g * pieces, 1) if g else full

    def line_of(n):
        return lined[pl.ds(n, 1), :]

    entry = {pairs[n]: line_of(n) + float(pairs[n][0] == pairs[n][1]) for n in range(len(pairs))}
    side = [line_of(len(pairs) + a) for a in range(BASES)]
    inverse = [None] * BASES
    for k in range(BASES):
        inverse[k] = 1.0 / entry[k, k]
        for i in range(k + 1, BASES):
            factor = entry[k, i] * inverse[k]
            for c in range(i, BASES):
                entry[i, c] = entry[i, c] - factor * entry[k, c]
            side[i] = side[i] - factor * side[k]
    for k in reversed(range(BASES)):
        for c in range(k + 1, BASES):
            side[k] = side[k] - entry[k, c] * side[c]
        side[k] = side[k] * inverse[k]
    found = jnp.zeros((8, LANES), F32)
    for a in range(BASES):
        found = found + jnp.where(iota((8, LANES), 0) == a, side[a], 0.0)
    high = found.astype(BF16).astype(F32)
    low = found - high
    both = jnp.concatenate([high, low], axis=0)[:, :pieces].astype(BF16)
    spread = tn(both, e3)
    for k in range(pieces):
        mixers[k // cap, pl.ds(k % cap * TILE, TILE), :] = jnp.where(
            diagonal, spread[k : k + 1], 0.0
        ).astype(BF16)

    for copy in exchanges:
        copy.wait_send()
    for local in (False, True):
        @pl.when(owning == local)
        def _():
            if halves - local:
                wait_for(sum_send, (halves - local) * sum(size(c) for c in range(chunks)))
    for sides in range(3 if strips > 2 else 2):
        mains = (bands * visits - 1) * (distinct + 1) * rows
        edges = bands * visits * distinct * sides * TILE

        @pl.when(owning & (reach == sides + 1))
        def _():
            wait_for(template_send, mains + edges)


def finish(coadd_in, image_s, basis, mixers, order, coadd_out, diff_out, diff_v, out_sem):
    distinct = basis.shape[0]
    blocks, pieces, _, cols = image_s.shape
    cap = pieces // distinct
    stores = [pltpu.make_async_copy(coadd_in, coadd_out.at[0, 0], out_sem.at[0])]
    stores[0].start()
    places = [order[0, k] for k in range(pieces)]
    for t in range(blocks):
        lanes = pl.ds(t * cols, cols)
        for d in range(distinct):
            planes = basis[d, :, lanes]
            fitted = nn(mixers[d], jnp.concatenate([planes, planes], axis=0))
            for k in range(cap):
                value = image_s[t, d * cap + k].astype(F32) - fitted[k * TILE : (k + 1) * TILE]
                diff_v[t, places[d * cap + k]] = value.astype(BF16)
        copy = pltpu.make_async_copy(
            diff_v.at[t], diff_out.at[0, :, pl.ds(t * TILE, TILE), :], out_sem.at[1 + t]
        )
        copy.start()
        stores.append(copy)
    for copy in stores:
        copy.wait()


def body(visits, strips, bands, images, mask_bits, visit_weight, intersection, patch_owner):
    _, pieces, rows, cols = images.shape
    blocks = rows // TILE
    halves = cols // LANES
    distinct = max(1, patch_owner.shape[0] // 2)
    cap = pieces // distinct
    taps = kernel_taps()
    width = -(-max(LANES, cols, rows + 2 * TILE) // LANES) * LANES
    tables = jnp.asarray(np.concatenate([
        np.pad(part, ((0, 0), (0, width - part.shape[1])))
        for part in (
            np.transpose(band_matrix(taps, cols, cols, HALF), (0, 2, 1)).reshape(3 * cols, cols),
            band_matrix(taps, rows, rows + 2 * TILE, HALF - TILE).reshape(3 * rows, -1),
        )
    ]), BF16)
    hbm = pl.BlockSpec(memory_space=pltpu.HBM)
    vmem = pl.BlockSpec(memory_space=pltpu.VMEM)
    dma = pltpu.SemaphoreType.DMA
    cross = intersection.reshape(1, pieces)
    others = max(1, strips - 1)
    chunks = 2
    parcel = distinct * 2 * rows // chunks + TILE
    lines = -(-(len(pairs) + BASES) // 8) * 8
    middle = pl.pallas_call(
        functools.partial(kernel, visits, strips, bands, distinct),
        out_shape=(
            jax.ShapeDtypeStruct((rows, cols), BF16),
            jax.ShapeDtypeStruct((blocks, pieces, TILE, cols), BF16),
            jax.ShapeDtypeStruct((distinct, BASES * TILE, blocks * cols), BF16),
            jax.ShapeDtypeStruct((distinct, cap * TILE, 2 * BASES * TILE), BF16),
            jax.ShapeDtypeStruct((1, LANES), jnp.int32),
        ),
        in_specs=[hbm, hbm, hbm, hbm, hbm, hbm],
        out_specs=(vmem, vmem, vmem, vmem, vmem),
        scratch_shapes=[
            pltpu.VMEM((pieces, rows, cols), jnp.int32),
            pltpu.VMEM((pieces, rows, cols), BF16),
            pltpu.VMEM(tables.shape, BF16),
            pltpu.VMEM((1, pieces), BF16),
            pltpu.SMEM((1, pieces), jnp.int32),
            pltpu.SMEM(patch_owner.shape, jnp.int32),
            pltpu.VMEM((pieces, TILE, blocks * cols), BF16),
            pltpu.VMEM((pieces, TILE, blocks * cols), BF16),
            pltpu.VMEM((distinct, blocks * cols, cap * TILE), BF16),
            pltpu.VMEM((distinct, blocks * cols, cap * TILE), BF16),
            pltpu.VMEM((halves, chunks, parcel, LANES), BF16),
            pltpu.VMEM((bands * chunks * visits * parcel, LANES), BF16),
            pltpu.VMEM((bands, visits, rows, LANES), BF16),
            pltpu.VMEM((bands, visits, distinct, rows, LANES), BF16),
            pltpu.VMEM((halves, distinct, rows + 2 * TILE, LANES), BF16),
            pltpu.VMEM((halves, rows, LANES), BF16),
            pltpu.VMEM((distinct, len(pairs) * TILE, blocks * cols), BF16),
            pltpu.VMEM((8, LANES), F32),
            pltpu.VMEM((others, 8, LANES), F32),
            pltpu.VMEM((lines, LANES), F32),
            dma((3,)),
            dma((2, 2)),
            dma,
            dma,
            dma((bands, chunks)),
            dma,
            dma,
            dma,
            dma,
            dma,
        ],
        compiler_params=pltpu.CompilerParams(
            collective_id=0, has_side_effects=True, vmem_limit_bytes=40_000_000
        ),
        name="coadd_solve",
    )(*(
        pltpu.with_memory_space_constraint(part, pltpu.HBM)
        for part in (images, mask_bits, visit_weight, cross, patch_owner, tables)
    ))
    return pl.pallas_call(
        finish,
        out_shape=(
            jax.ShapeDtypeStruct((1, 1, rows, cols), BF16),
            jax.ShapeDtypeStruct(images.shape, BF16),
        ),
        in_specs=[vmem, vmem, vmem, vmem, vmem],
        out_specs=(hbm, hbm),
        scratch_shapes=[
            pltpu.VMEM((blocks, pieces, TILE, cols), BF16),
            dma((1 + blocks,)),
        ],
        compiler_params=pltpu.CompilerParams(vmem_limit_bytes=40 * 1024 * 1024),
        name="difference",
    )(*middle)


def solution(mesh):
    in_specs = (
        P("band", ("groups", "visit"), "strip", None),
        P("band", ("groups", "visit"), "strip", None),
        P("band", ("groups", "visit")),
        P(("groups", "visit"), None),
        P("groups"),
    )
    out_specs = (
        P("band", ("groups", "visit"), "strip", None),
        P("band", ("groups", "visit"), "strip", None),
    )
    step = functools.partial(
        body, mesh.shape["visit"], mesh.shape["strip"], mesh.shape["band"]
    )
    return jax.shard_map(step, mesh=mesh, in_specs=in_specs, out_specs=out_specs, check_vma=False)
```

```python
import functools

import jax
import jax.numpy as jnp
import numpy as np
from jax import lax
from jax.experimental import pallas as pl
from jax.experimental.pallas import tpu as pltpu
from jax.sharding import PartitionSpec as P

BASES = 6
HALF = 9
TILE = 16
LANES = 128

basis_rows = (0, 0, 1, 0, 2, 1)
basis_cols = (0, 1, 0, 2, 0, 1)
pairs = tuple((a, c) for a in range(BASES) for c in range(a, BASES))
MESH = pl.DeviceIdType.MESH
F32 = jnp.float32
BF16 = jnp.bfloat16


def kernel_taps():
    offsets = np.arange(2 * HALF + 1).astype(np.float32) - HALF
    gaussian = np.exp(-offsets * offsets / np.float32(18.0))
    centre = np.sum(offsets * offsets * gaussian * gaussian) / np.sum(gaussian * gaussian)
    table = np.stack([gaussian, offsets * gaussian, (offsets * offsets - centre) * gaussian])
    table = table / np.sqrt(np.sum(table * table, axis=1, keepdims=True))
    return table.astype(BF16).astype(np.float32)


def band_matrix(table, lead, trail, displace):
    index = np.arange(trail)[None, :] - np.arange(lead)[:, None] + displace
    inside = (index >= 0) & (index <= 2 * HALF)
    return np.where(inside[None], table[:, np.clip(index, 0, 2 * HALF)], 0.0)


def iota(shape, dim):
    return lax.broadcasted_iota(jnp.int32, shape, dim)


def nn(a, b):
    return jnp.dot(a, b, preferred_element_type=F32)


def nt(a, b):
    return lax.dot_general(a, b, (((1,), (1,)), ((), ())), preferred_element_type=F32)


def tn(a, b):
    return lax.dot_general(a, b, (((0,), (0,)), ((), ())), preferred_element_type=F32)


def each(count, step):
    if count <= 4:
        for k in range(count):
            step(k)
    else:
        def body(k, carry):
            step(k)
            return carry

        lax.fori_loop(0, count, body, 0)


def thirds(value):
    high = value.astype(BF16)
    rest = value - high.astype(F32)
    middle = rest.astype(BF16)
    low = (rest - middle.astype(F32)).astype(BF16)
    return jnp.concatenate([high, middle, low], axis=0)


def kernel(
    visits, strips, bands, distinct,
    images, masks, weight_in, cross_in, owner_in, table_in,
    coadd_out, image_s, basis, mixers, order_out,
    mask_v, image_v, tables, weight, cross, owner, use, use_image, turned, turned_image, send, recv,
    patches, chosen, template_v, owned, prods, small, small_in, lined,
    first_sem, in_sem, const_sem, sum_send, sum_recv, template_send, template_recv, owned_recv,
    st_send, st_recv,
):
    pieces, rows, cols = images.shape[1:]
    blocks = rows // TILE
    chunks = sum_recv.shape[1]
    parts = in_sem.shape[1]
    chunk = rows // chunks
    span = pieces * TILE
    cap = pieces // distinct
    halves = cols // LANES
    lead = (visits - halves) // 2
    last = bands - 1
    sheet = distinct * 2 * chunk
    parcel = sheet + TILE
    me = lax.axis_index("visit")
    strip = lax.axis_index("strip")
    band = lax.axis_index("band")
    above = strip > 0
    below = strip < strips - 1
    mine = me - lead
    late = me * 2 >= visits
    central = (me >= lead) & (me < lead + halves)
    owning = central & (band == last)
    reach = 1 + above.astype(jnp.int32) + below.astype(jnp.int32)

    def visit_all(act, others_only=False):
        if visits > 4:
            each(visits - others_only, lambda k: act(lax.rem(me + others_only + k, visits)))
            return
        hops = sorted(range(visits), key=lambda k: (abs(k - visits // 2), -k))
        for k in hops:
            if k or not others_only:
                act(lax.rem(me + jnp.where(late, visits - k, k), visits))

    barrier = pltpu.get_barrier_semaphore()

    def greet(v, hop, b):
        target = {"visit": v, "strip": lax.rem(strip + hop, strips), "band": b}
        pl.semaphore_signal(barrier, inc=1, device_id=target, device_id_type=MESH)

    def near(hop, step):
        if hop == 0:
            step()
        elif hop == 1 and strips == 2:
            step()
        elif hop == 1:
            pl.when(below)(step)
        elif hop == strips - 1:
            pl.when(above)(step)

    def adjoining(hop):
        if hop in (0, 1) and strips == 2:
            return jnp.bool_(True)
        return below if hop == 1 else (above if hop == strips - 1 else jnp.bool_(False))

    @pl.when(owning)
    def _():
        for b in range(bands):
            visit_all(lambda v: greet(v, 0, b), b == last)
        for hop in sorted({1 % strips, strips - 1} - {0}):
            def greet_owners():
                for h in range(halves):
                    greet(lead + h, hop, last)

            near(hop, greet_owners)
            if strips > 2:
                pl.when(jnp.logical_not(adjoining(hop)))(functools.partial(greet, me, hop, band))
        for hop in range(2, strips - 1):
            greet(me, hop, band)

    firsts = [
        pltpu.make_async_copy(cross_in, cross, first_sem.at[0]),
        pltpu.make_async_copy(owner_in, owner, first_sem.at[1]),
        pltpu.make_async_copy(weight_in, weight, first_sem.at[2]),
    ]
    for copy in firsts:
        copy.start()

    loads = []
    for k in range(parts):
        part = pl.ds(k * rows // parts, rows // parts)
        loads.append((
            pltpu.make_async_copy(masks.at[0, :, part, :], mask_v.at[:, part, :], in_sem.at[0, k]),
            pltpu.make_async_copy(images.at[0, :, part, :], image_v.at[:, part, :], in_sem.at[1, k]),
        ))
        for copy in loads[k]:
            copy.start()

    @pl.when(jnp.logical_not(owning))
    def _():
        for hop in sorted({0, 1 % strips, strips - 1}):
            def greet_owners():
                for h in range(halves):
                    greet(lead + h, hop, last)

            near(hop, greet_owners)
        for hop in range(1, strips):
            greet(me, hop, band)

    constants = pltpu.make_async_copy(table_in, tables, const_sem)
    constants.start()

    for copy in firsts:
        copy.wait()
    seats = [owner[cross[0, j]] for j in range(pieces)]
    slots = [jnp.int32(0)] * distinct
    rank = jnp.int32(0)
    for q in range(visits):
        present = jnp.int32(0)
        for j in range(pieces):
            present = present | jnp.where(seats[j] == q, 1, 0)
        for d in range(distinct):
            slots[d] = slots[d] + jnp.where((present == 1) & (rank == d), q, 0)
        rank = rank + present

    position = jnp.zeros((1, pieces), jnp.int32)
    for j in range(pieces):
        position = position + jnp.where(iota((1, pieces), 1) == j, seats[j], 0)
    e2 = iota((pieces, span), 0) == jnp.right_shift(iota((pieces, span), 1), 4)
    e2 = e2.astype(F32).astype(BF16)
    pair = jnp.where(
        iota((8, pieces), 0) == 0, weight[...].astype(F32), position.astype(F32)
    ).astype(BF16)
    wide = nn(pair, e2)
    same = (iota((TILE, span), 0) & (TILE - 1)) == (iota((TILE, span), 1) & (TILE - 1))
    adder = jnp.concatenate([
        jnp.where(same & (wide[1:2] == lax.convert_element_type(slots[d], F32)), wide[0:1], 0.0)
        for d in range(distinct)
    ], axis=0).astype(BF16)
    names = jnp.zeros((TILE, LANES), jnp.int32)
    for d in range(distinct):
        names = names + jnp.where(iota((TILE, LANES), 0) == d, slots[d], 0)
    for h in range(halves):
        send[h, 0, pl.ds(sheet, TILE), :] = names.astype(F32).astype(BF16)

    def parcel_at(b, c, v):
        return pl.multiple_of(((b * chunks + c) * visits + v) * parcel, TILE)

    def size(c):
        return parcel if c == 0 else sheet

    def some(count):
        return recv.at[pl.ds(0, count), :]

    def sum_copy(h, c):
        return pltpu.make_async_remote_copy(
            src_ref=send.at[h, c, pl.ds(0, size(c)), :],
            dst_ref=recv.at[pl.ds(parcel_at(band, c, me), size(c)), :],
            send_sem=sum_send, recv_sem=sum_recv.at[band, c],
            device_id={"visit": lead + h, "band": last}, device_id_type=MESH,
        )

    def template_copy(b, h, v, c):
        return pltpu.make_async_remote_copy(
            src_ref=chosen.at[b, v, :, pl.ds(c * chunk, chunk), :],
            dst_ref=template_v.at[h, :, pl.ds(TILE + c * chunk, chunk), :],
            send_sem=template_send, recv_sem=template_recv,
            device_id={"visit": v, "band": b}, device_id_type=MESH,
        )

    def edge_copy(way, b, h, v):
        step, source, target = ((1, rows - TILE, 0), (strips - 1, 0, rows + TILE))[way]
        return pltpu.make_async_remote_copy(
            src_ref=chosen.at[b, v, :, pl.ds(source, TILE), :],
            dst_ref=template_v.at[h, :, pl.ds(target, TILE), :],
            send_sem=template_send, recv_sem=template_recv,
            device_id={"visit": v, "strip": lax.rem(strip + step, strips), "band": b},
            device_id_type=MESH,
        )

    def owned_copy(b, h, v):
        return pltpu.make_async_remote_copy(
            src_ref=patches.at[b, v], dst_ref=owned.at[h],
            send_sem=template_send, recv_sem=owned_recv,
            device_id={"visit": v, "band": b}, device_id_type=MESH,
        )

    def wait_for(sem, count):
        pltpu.make_async_copy(some(count), some(count), sem).wait()

    def partial(c):
        if c * parts % chunks == 0:
            for copy in loads[c * parts // chunks]:
                copy.wait()
        for t in range(c * chunk // TILE, (c + 1) * chunk // TILE):
            piece_rows = pl.ds(t * TILE, TILE)
            lanes = pl.ds(t * cols, cols)
            usable = (mask_v[:, piece_rows, :].reshape(span, cols) & 3) != 3
            usable = usable.astype(F32).astype(BF16)
            masked = usable * image_v[:, piece_rows, :].reshape(span, cols)
            use[:, :, lanes] = usable.reshape(pieces, TILE, cols)
            use_image[:, :, lanes] = masked.reshape(pieces, TILE, cols)
            for part, value in enumerate((masked, usable)):
                total = nn(adder, value).astype(BF16)
                for d in range(distinct):
                    for h in range(halves):
                        at = (d * 2 + part) * chunk + t * TILE - c * chunk
                        send[h, c, pl.ds(at, TILE), :] = total[
                            d * TILE : (d + 1) * TILE, h * LANES : (h + 1) * LANES
                        ]

    met = jnp.where(
        owning, visits * bands * reach - 1 + strips - reach, halves + strips - 1
    )
    for c in range(chunks):
        partial(c)
        if c == 0:
            pl.semaphore_wait(barrier, met)
        for k in range(halves):
            h = jnp.where(late, k, halves - 1 - k)
            pl.when(jnp.logical_not(owning & (mine == h)))(sum_copy(h, c).start)

    @pl.when(jnp.logical_not(above))
    def _():
        template_v[:, :, pl.ds(0, TILE), :] = jnp.zeros((halves, distinct, TILE, LANES), BF16)

    @pl.when(jnp.logical_not(below))
    def _():
        template_v[:, :, pl.ds(rows + TILE, TILE), :] = jnp.zeros(
            (halves, distinct, TILE, LANES), BF16
        )

    def reduce(b, c):
        if b == last:
            recv[pl.ds(parcel_at(b, c, me), parcel), :] = send[mine, c]
        wait_for(sum_recv.at[b, c], (visits if b != last else visits - 1) * size(c))

        def id_tile(v, d):
            names = recv[pl.ds(parcel_at(b, 0, v) + sheet, TILE), :].astype(F32)
            return jnp.broadcast_to(names[d : d + 1], (TILE, LANES))

        def value(v, d, part, t):
            at = (d * 2 + part) * chunk + t * TILE - c * chunk
            start = pl.multiple_of(parcel_at(b, c, v) + at, TILE)
            return recv[pl.ds(start, TILE), :].astype(F32)

        def one_tile(t):
            piece_rows = pl.ds(t * TILE, TILE)
            if visits <= 4:
                tiles = [[id_tile(v, d) for d in range(distinct)] for v in range(visits)]
                finals = []
                for q in range(visits):
                    numerator = jnp.zeros((TILE, LANES), F32)
                    denominator = jnp.zeros((TILE, LANES), F32)
                    for v in range(visits):
                        for d in range(distinct):
                            here = tiles[v][d] == float(q)
                            numerator += jnp.where(here, value(v, d, 0, t), 0.0)
                            denominator += jnp.where(here, value(v, d, 1, t), 0.0)
                    final = numerator / jnp.maximum(denominator, 1.0)
                    patches[b, q, piece_rows, :] = final.astype(BF16)
                    finals.append(final)
                for v in range(visits):
                    for d in range(distinct):
                        picked = finals[0]
                        for q in range(1, visits):
                            picked = jnp.where(tiles[v][d] == float(q), finals[q], picked)
                        chosen[b, v, d, piece_rows, :] = picked.astype(BF16)
                return

            def one_patch(q):
                number = lax.convert_element_type(q, F32)

                def add(v, carry):
                    numerator, denominator = carry
                    for d in range(distinct):
                        here = id_tile(v, d) == number
                        numerator += jnp.where(here, value(v, d, 0, t), 0.0)
                        denominator += jnp.where(here, value(v, d, 1, t), 0.0)
                    return numerator, denominator

                zero = jnp.zeros((TILE, LANES), F32)
                numerator, denominator = lax.fori_loop(0, visits, add, (zero, zero))
                final = numerator / jnp.maximum(denominator, 1.0)
                patches[b, q, piece_rows, :] = final.astype(BF16)

            def pick(v):
                for d in range(distinct):
                    tile = id_tile(v, d)

                    def better(q, picked):
                        final = patches[b, q, piece_rows, :].astype(F32)
                        return jnp.where(tile == lax.convert_element_type(q, F32), final, picked)

                    picked = lax.fori_loop(0, visits, better, jnp.zeros((TILE, LANES), F32))
                    chosen[b, v, d, piece_rows, :] = picked.astype(BF16)

            each(visits, one_patch)
            each(visits, pick)

        for t in range(c * chunk // TILE, (c + 1) * chunk // TILE):
            one_tile(t)

        if c == chunks - 1:
            @pl.when(below)
            def _():
                visit_all(lambda v: edge_copy(0, b, mine, v).start())

        if c == 0:
            @pl.when(above)
            def _():
                visit_all(lambda v: edge_copy(1, b, mine, v).start())

        visit_all(lambda v: template_copy(b, mine, v, c).start(), b == last)

    @pl.when(owning)
    def _():
        for b in range(bands):
            for c in range(chunks):
                reduce(b, c)
        template_v[mine, :, pl.ds(TILE, rows), :] = chosen[last, me]
        for b in range(bands):
            visit_all(lambda v: owned_copy(b, mine, v).start(), b == last)
        owned[mine] = patches[last, me]

    places = []
    for d in range(distinct):
        count = jnp.int32(0)
        found = [jnp.int32(0)] * cap
        for j in range(pieces):
            hit = seats[j] == slots[d]
            for k in range(cap):
                found[k] = found[k] + jnp.where(hit & (count == k), j, 0)
            count = count + jnp.where(hit, 1, 0)
        places += found
    order = jnp.zeros((1, LANES), jnp.int32)
    for k in range(pieces):
        order = order + jnp.where(iota((1, LANES), 1) == k, places[k], 0)
        for t in range(blocks):
            image_s[t, k] = image_v[places[k], pl.ds(t * TILE, TILE), :]
    order_out[...] = order
    for d in range(distinct):
        for t in range(blocks):
            lanes = pl.ds(t * cols, cols)
            for source, target in ((use, turned), (use_image, turned_image)):
                stack = [source[places[d * cap + k], :, lanes] for k in range(cap)]
                target[d, lanes, :] = jnp.transpose(jnp.concatenate(stack, axis=0))
    constants.wait()

    up_top = BASES // 2 * cols
    vertical = tables[pl.ds(up_top, 3 * rows), pl.ds(0, rows + 2 * TILE)]

    def across(c):
        return tables[pl.ds(c * cols, cols), pl.ds(0, cols)]

    wide_n = len(pairs) * TILE
    wide_b = BASES * TILE
    lines = lined.shape[0]

    for local in (False, True):
        for sides in range(3 if strips > 2 else 2):
            count = distinct * ((halves - local) * rows + halves * sides * TILE)

            @pl.when((owning == local) & (reach == sides + 1))
            def _():
                if count:
                    wait_for(template_recv, count)

    corner = iota((1, TILE, cap * TILE), 1) == (iota((1, TILE, cap * TILE), 2) & (TILE - 1))
    smooth = nn(vertical, jnp.concatenate(
        [template_v[h, d] for d in range(distinct) for h in range(halves)], axis=1
    )).astype(BF16)
    planes = [[None] * BASES for _ in range(distinct)]
    for c in range(3):
        taken = [a for a in range(BASES) if basis_cols[a] == c]
        height = len(taken) * rows
        product = nn(jnp.concatenate(
            [smooth[:height, d * cols : (d + 1) * cols] for d in range(distinct)], axis=0
        ), across(c)).astype(BF16)
        for d in range(distinct):
            for a in taken:
                top = d * height + basis_rows[a] * rows
                planes[d][a] = product[top : top + rows]
    for d in range(distinct):
        for a in range(BASES):
            for t in range(blocks):
                basis[d, pl.ds(a * TILE, TILE), pl.ds(t * cols, cols)] = planes[d][a][
                    t * TILE : (t + 1) * TILE
                ]
        for n, (a, c) in enumerate(pairs):
            product = planes[d][a] * planes[d][c]
            for t in range(blocks):
                prods[d, pl.ds(n * TILE, TILE), pl.ds(t * cols, cols)] = product[
                    t * TILE : (t + 1) * TILE
                ]

    groups = lines // 8
    folded = []
    for d in range(distinct):
        sums = jnp.concatenate([
            nn(prods[d], turned[d]),
            nn(basis[d], turned_image[d]),
            jnp.zeros((lines * TILE - wide_n - wide_b, cap * TILE), F32),
        ], axis=0).reshape(lines, TILE, cap * TILE)
        folded.append(jnp.sum(jnp.where(corner, sums, 0.0), axis=1))
    collect = jnp.concatenate([
        jnp.right_shift(iota((cap * TILE, LANES), 0), 4) + d * cap for d in range(distinct)
    ], axis=0)
    collect = (collect == iota(collect.shape, 1)).astype(F32).astype(BF16)
    gathered = nn(thirds(jnp.concatenate(folded, axis=1)), collect)
    system = sum(gathered[k * lines : (k + 1) * lines] for k in range(3))
    small[...] = sum(
        pltpu.roll(system[g * 8 : (g + 1) * 8], g * pieces, 1) if g else system[:8]
        for g in range(groups)
    )
    exchanges = []
    for hop in range(1, strips):
        exchanges.append(pltpu.make_async_remote_copy(
            src_ref=small, dst_ref=small_in.at[hop - 1],
            send_sem=st_send, recv_sem=st_recv,
            device_id={"strip": lax.rem(strip + hop, strips)}, device_id_type=MESH,
        ))
    for copy in exchanges:
        copy.start()

    wide_c = 2 * wide_b
    column = iota((16, wide_c), 1)
    source = jnp.where(
        column < wide_b, jnp.right_shift(column, 4), jnp.right_shift(column - wide_b, 4) + 8
    )
    e3 = (source == iota((16, wide_c), 0)).astype(F32).astype(BF16)
    diagonal = iota((TILE, wide_c), 0) == (iota((TILE, wide_c), 1) & (TILE - 1))

    for local in (False, True):
        @pl.when(owning == local)
        def _():
            if halves - local:
                wait_for(owned_recv, (halves - local) * rows)
    for h in range(halves):
        coadd_out[:, pl.ds(h * LANES, LANES)] = owned[h]

    if exchanges:
        pltpu.make_async_copy(small_in, small_in, st_recv).wait()

    full = small[...]
    for hop in range(1, strips):
        full = full + small_in[hop - 1]
    for g in range(groups):
        lined[pl.ds(g * 8, 8), :] = pltpu.roll(full, LANES - g * pieces, 1) if g else full

    def line_of(n):
        return lined[pl.ds(n, 1), :]

    entry = {pairs[n]: line_of(n) + float(pairs[n][0] == pairs[n][1]) for n in range(len(pairs))}
    side = [line_of(len(pairs) + a) for a in range(BASES)]
    inverse = [None] * BASES
    for k in range(BASES):
        inverse[k] = 1.0 / entry[k, k]
        for i in range(k + 1, BASES):
            factor = entry[k, i] * inverse[k]
            for c in range(i, BASES):
                entry[i, c] = entry[i, c] - factor * entry[k, c]
            side[i] = side[i] - factor * side[k]
    for k in reversed(range(BASES)):
        for c in range(k + 1, BASES):
            side[k] = side[k] - entry[k, c] * side[c]
        side[k] = side[k] * inverse[k]
    found = jnp.zeros((8, LANES), F32)
    for a in range(BASES):
        found = found + jnp.where(iota((8, LANES), 0) == a, side[a], 0.0)
    high = found.astype(BF16).astype(F32)
    low = found - high
    both = jnp.concatenate([high, low], axis=0)[:, :pieces].astype(BF16)
    spread = tn(both, e3)
    for k in range(pieces):
        mixers[k // cap, pl.ds(k % cap * TILE, TILE), :] = jnp.where(
            diagonal, spread[k : k + 1], 0.0
        ).astype(BF16)

    for copy in exchanges:
        copy.wait_send()
    for local in (False, True):
        @pl.when(owning == local)
        def _():
            if halves - local:
                wait_for(sum_send, (halves - local) * sum(size(c) for c in range(chunks)))
    for sides in range(3 if strips > 2 else 2):
        mains = (bands * visits - 1) * (distinct + 1) * rows
        edges = bands * visits * distinct * sides * TILE

        @pl.when(owning & (reach == sides + 1))
        def _():
            wait_for(template_send, mains + edges)


def finish(coadd_in, image_s, basis, mixers, order, coadd_out, diff_out, diff_v, out_sem):
    distinct = basis.shape[0]
    blocks, pieces, _, cols = image_s.shape
    cap = pieces // distinct
    stores = [pltpu.make_async_copy(coadd_in, coadd_out.at[0, 0], out_sem.at[0])]
    stores[0].start()
    places = [order[0, k] for k in range(pieces)]
    for t in range(blocks):
        lanes = pl.ds(t * cols, cols)
        for d in range(distinct):
            planes = basis[d, :, lanes]
            fitted = nn(mixers[d], jnp.concatenate([planes, planes], axis=0))
            for k in range(cap):
                value = image_s[t, d * cap + k].astype(F32) - fitted[k * TILE : (k + 1) * TILE]
                diff_v[t, places[d * cap + k]] = value.astype(BF16)
        copy = pltpu.make_async_copy(
            diff_v.at[t], diff_out.at[0, :, pl.ds(t * TILE, TILE), :], out_sem.at[1]
        )
        copy.start()
    stores[0].wait()
    pltpu.make_async_copy(diff_v, diff_v, out_sem.at[1]).wait()


def body(visits, strips, bands, images, mask_bits, visit_weight, intersection, patch_owner):
    _, pieces, rows, cols = images.shape
    blocks = rows // TILE
    halves = cols // LANES
    distinct = max(1, patch_owner.shape[0] // 2)
    cap = pieces // distinct
    taps = kernel_taps()
    width = -(-max(LANES, cols, rows + 2 * TILE) // LANES) * LANES
    tables = jnp.asarray(np.concatenate([
        np.pad(part, ((0, 0), (0, width - part.shape[1])))
        for part in (
            np.transpose(band_matrix(taps, cols, cols, HALF), (0, 2, 1)).reshape(3 * cols, cols),
            band_matrix(taps, rows, rows + 2 * TILE, HALF - TILE).reshape(3 * rows, -1),
        )
    ]), BF16)
    hbm = pl.BlockSpec(memory_space=pltpu.HBM)
    vmem = pl.BlockSpec(memory_space=pltpu.VMEM)
    dma = pltpu.SemaphoreType.DMA
    cross = intersection.reshape(1, pieces)
    others = max(1, strips - 1)
    chunks = 4
    parcel = distinct * 2 * rows // chunks + TILE
    lines = -(-(len(pairs) + BASES) // 8) * 8
    middle = pl.pallas_call(
        functools.partial(kernel, visits, strips, bands, distinct),
        out_shape=(
            jax.ShapeDtypeStruct((rows, cols), BF16),
            jax.ShapeDtypeStruct((blocks, pieces, TILE, cols), BF16),
            jax.ShapeDtypeStruct((distinct, BASES * TILE, blocks * cols), BF16),
            jax.ShapeDtypeStruct((distinct, cap * TILE, 2 * BASES * TILE), BF16),
            jax.ShapeDtypeStruct((1, LANES), jnp.int32),
        ),
        in_specs=[hbm, hbm, hbm, hbm, hbm, hbm],
        out_specs=(vmem, vmem, vmem, vmem, vmem),
        scratch_shapes=[
            pltpu.VMEM((pieces, rows, cols), jnp.int32),
            pltpu.VMEM((pieces, rows, cols), BF16),
            pltpu.VMEM(tables.shape, BF16),
            pltpu.VMEM((1, pieces), BF16),
            pltpu.SMEM((1, pieces), jnp.int32),
            pltpu.SMEM(patch_owner.shape, jnp.int32),
            pltpu.VMEM((pieces, TILE, blocks * cols), BF16),
            pltpu.VMEM((pieces, TILE, blocks * cols), BF16),
            pltpu.VMEM((distinct, blocks * cols, cap * TILE), BF16),
            pltpu.VMEM((distinct, blocks * cols, cap * TILE), BF16),
            pltpu.VMEM((halves, chunks, parcel, LANES), BF16),
            pltpu.VMEM((bands * chunks * visits * parcel, LANES), BF16),
            pltpu.VMEM((bands, visits, rows, LANES), BF16),
            pltpu.VMEM((bands, visits, distinct, rows, LANES), BF16),
            pltpu.VMEM((halves, distinct, rows + 2 * TILE, LANES), BF16),
            pltpu.VMEM((halves, rows, LANES), BF16),
            pltpu.VMEM((distinct, len(pairs) * TILE, blocks * cols), BF16),
            pltpu.VMEM((8, LANES), F32),
            pltpu.VMEM((others, 8, LANES), F32),
            pltpu.VMEM((lines, LANES), F32),
            dma((3,)),
            dma((2, 2)),
            dma,
            dma,
            dma((bands, chunks)),
            dma,
            dma,
            dma,
            dma,
            dma,
        ],
        compiler_params=pltpu.CompilerParams(
            collective_id=0, has_side_effects=True, vmem_limit_bytes=40_000_000
        ),
        name="coadd_solve",
    )(*(
        pltpu.with_memory_space_constraint(part, pltpu.HBM)
        for part in (images, mask_bits, visit_weight, cross, patch_owner, tables)
    ))
    return pl.pallas_call(
        finish,
        out_shape=(
            jax.ShapeDtypeStruct((1, 1, rows, cols), BF16),
            jax.ShapeDtypeStruct(images.shape, BF16),
        ),
        in_specs=[vmem, vmem, vmem, vmem, vmem],
        out_specs=(hbm, hbm),
        scratch_shapes=[
            pltpu.VMEM((blocks, pieces, TILE, cols), BF16),
            dma((2,)),
        ],
        compiler_params=pltpu.CompilerParams(vmem_limit_bytes=40 * 1024 * 1024),
        name="difference",
    )(*middle)


def solution(mesh):
    in_specs = (
        P("band", ("groups", "visit"), "strip", None),
        P("band", ("groups", "visit"), "strip", None),
        P("band", ("groups", "visit")),
        P(("groups", "visit"), None),
        P("groups"),
    )
    out_specs = (
        P("band", ("groups", "visit"), "strip", None),
        P("band", ("groups", "visit"), "strip", None),
    )
    step = functools.partial(
        body, mesh.shape["visit"], mesh.shape["strip"], mesh.shape["band"]
    )
    return jax.shard_map(step, mesh=mesh, in_specs=in_specs, out_specs=out_specs, check_vma=False)
```
